32 devices in a mesh: row: 4 (over y, x), col: 8 (over z, core).
Axes of the slice: x: 2, y: 2, z: 4, core: 2. Of those that a mesh axis runs over, the one named last changes fastest.
Arguments:
- velocities: bfloat16 [1024, 30720], P(None, 'row'), may hold values from -60 to 60, as said below
- modes_panel: bfloat16 [30720, 4096], P('row', 'col'), may hold values from -1 to 1
- atom_slot: int32 [10240], P('row'), may hold values from 0 to 2559, as said below
- lag_offsets: int32 [8], replicated, may hold values from 0 to 256, as said below
Outputs:
- correlations: float32 [8, 4096, 4096], P(None, 'row', 'col')
The draws below stay inside these ranges and needn't reach their ends.
Inputs may be any that keep to these rules, and one draw needn't show every extreme that they name: `velocities`: every snapshot row has its own scale. Within each aligned block of 2560 atoms, atom_slot is a permutation of 0 to 2559. `lag_offsets`: one of the lags equals 256.
All inputs are finite; a program needn't handle non-finite values.
Results may differ from the reference program's by a relative error of at most 0.0041.
Values may be sent and summed in bfloat16 or wider, within the bound.
No kernel may reach another device: no remote copies, remote signals or barrier semaphores. Data moves between devices by JAX's collectives and lax.ppermute only.
A program may use at most 128 MiB of HBM per device.

```python
import jax
import jax.numpy as jnp
from jax import lax

M = 4096
ATOM_DEV = 2560
S = 1024
LAGS = 8
NATOMS = 10240
COORDS = 30720
MAXLAG = 256


def draw_velocities(key, part):
    first, second = jax.random.split(jax.random.fold_in(key, 11))
    base = jnp.clip(jax.random.normal(first, (S, COORDS), jnp.float32), -6.0, 6.0)
    scales = jnp.exp(jax.random.uniform(second, (S, 1), jnp.float32, 0.0, jnp.log(10.0)))
    return jnp.clip(base * scales, -60.0, 60.0).astype(jnp.bfloat16)


def draw_modes_panel(key, part):
    first, second = jax.random.split(jax.random.fold_in(key, 23))
    ramp = jnp.arange(M, dtype=jnp.float32) / (M - 1)
    base = jnp.clip(jax.random.normal(first, (COORDS, M), jnp.float32), -6.0, 6.0)
    scales = jnp.exp(jnp.log(3.0) * ramp) * jax.random.uniform(second, (M,), jnp.float32, 0.7, 1.4)
    values = base * scales[None, :] * (1.0 / jnp.sqrt(jnp.float32(COORDS)))
    return jnp.clip(values, -1.0, 1.0).astype(jnp.bfloat16)


def draw_atom_slot(key, part):
    keys = jax.random.split(jax.random.fold_in(key, 37), NATOMS // ATOM_DEV)
    perms = jax.vmap(lambda single: jax.random.permutation(single, ATOM_DEV))(keys)
    return perms.reshape(NATOMS).astype(jnp.int32)


def draw_lag_offsets(key, part):
    first, second = jax.random.split(jax.random.fold_in(key, 41))
    values = jax.random.randint(first, (LAGS,), 0, MAXLAG, jnp.int32)
    where_top = jax.random.randint(second, (), 0, LAGS, jnp.int32)
    return jnp.where(jnp.arange(LAGS, dtype=jnp.int32) == where_top, MAXLAG, values).astype(jnp.int32)


def setup_inputs(seed: int = 0) -> dict:
    splits = jax.random.split(jax.random.key(seed), 5)
    velocities = draw_velocities(jax.random.fold_in(splits[4], 71), 0)
    modes_panel = draw_modes_panel(jax.random.fold_in(splits[4], 71), 0)
    atom_slot = draw_atom_slot(jax.random.fold_in(splits[4], 71), 0)
    lag_offsets = draw_lag_offsets(jax.random.fold_in(splits[4], 71), 0)
    return {"velocities": velocities, "modes_panel": modes_panel, "atom_slot": atom_slot, "lag_offsets": lag_offsets}


def reference(velocities, modes_panel, atom_slot, lag_offsets):
    block_start = jnp.arange(NATOMS, dtype=jnp.int32) // ATOM_DEV * ATOM_DEV
    chosen = (block_start + atom_slot).astype(jnp.int32)
    per_atom = modes_panel.reshape(NATOMS, 3, M)
    panel_ordered = jnp.take(per_atom, chosen, axis=0).reshape(COORDS, M)
    projected = jnp.dot(velocities, panel_ordered, preferred_element_type=jnp.float32)
    energy = lax.optimization_barrier(jnp.sum(projected * projected, axis=1))
    normalized = (projected * lax.rsqrt(energy / M + 1e-06)[:, None]).astype(jnp.bfloat16)
    padded = jnp.concatenate([normalized, jnp.zeros((MAXLAG, M), jnp.bfloat16)], axis=0)

    def one_lag(offset):
        shifted = lax.dynamic_slice_in_dim(padded, offset.astype(jnp.int32), S, 0)
        product = lax.dot_general(normalized, shifted, (((0,), (0,)), ((), ())), preferred_element_type=jnp.float32)
        return product * lax.rsqrt((S - offset).astype(jnp.float32))
    return lax.map(one_lag, lag_offsets)
```

```python
import functools

import jax
import jax.numpy as jnp
from jax import lax
from jax.experimental import pallas as pl
from jax.experimental.pallas import tpu as pltpu
from jax.sharding import PartitionSpec as P

MAXLAG = 256
LANES = 128
ROWS = 8
GROUP = 16

epsilon = 1e-06


def swap(block, axis, offset):
    size = lax.axis_size(axis)
    return lax.ppermute(block, axis, [(i, i ^ offset) for i in range(size)])


def reorder_kernel(slot, panel, out, staged, source, in_sems, ordered, out_sem, *, chunk):
    depth, width = panel.shape
    blocks = width // LANES
    copies = [
        pltpu.make_async_copy(
            panel.at[pl.ds(c * chunk, chunk), :], staged.at[pl.ds(c * chunk, chunk), :], in_sems.at[c]
        )
        for c in range(depth // chunk)
    ]
    for copy in copies:
        copy.start()
    for c, copy in enumerate(copies):
        copy.wait()

        def widen(i, carry):
            first = pl.multiple_of(c * chunk + i * 64, 64)
            for j in range(blocks):
                source[j, pl.ds(ROWS + first, 64), :] = staged[
                    pl.ds(first, 64), j * LANES : (j + 1) * LANES
                ].astype(jnp.float32)
            return carry

        lax.fori_loop(0, chunk // 64, widen, 0)
    row = lax.broadcasted_iota(jnp.int32, (ROWS, LANES), 0)

    def move(g, carry):
        base = [slot[g * GROUP + i] * 3 for i in range(GROUP)]
        for j in range(blocks):
            tiles = []
            for v in range(3 * GROUP // ROWS):
                tile = None
                for i in range(GROUP):
                    low = 3 * i - ROWS * v
                    if low + 3 <= 0 or low >= ROWS:
                        continue
                    piece = source[j, pl.ds(base[i] + (ROWS - low), ROWS), :]
                    tile = piece if tile is None else jnp.where(row >= low, piece, tile)
                tiles.append(tile)
            ordered[
                pl.ds(pl.multiple_of(g * 3 * GROUP, GROUP), 3 * GROUP), j * LANES : (j + 1) * LANES
            ] = jnp.concatenate(tiles, axis=0).astype(jnp.bfloat16)
        return carry

    lax.fori_loop(0, slot.shape[0] // GROUP, move, 0)
    copy = pltpu.make_async_copy(ordered, out, out_sem)
    copy.start()
    copy.wait()


def reorder(panel, slot):
    depth, width = panel.shape
    chunk = depth // 10
    return pl.pallas_call(
        functools.partial(reorder_kernel, chunk=chunk),
        out_shape=jax.ShapeDtypeStruct((depth, width), jnp.bfloat16),
        grid_spec=pltpu.PrefetchScalarGridSpec(
            num_scalar_prefetch=1,
            grid=(1,),
            in_specs=[pl.BlockSpec(memory_space=pl.ANY)],
            out_specs=pl.BlockSpec(memory_space=pl.ANY),
            scratch_shapes=[
                pltpu.VMEM((depth, width), jnp.bfloat16),
                pltpu.VMEM((width // LANES, depth + 2 * ROWS, LANES), jnp.float32),
                pltpu.SemaphoreType.DMA((depth // chunk,)),
                pltpu.VMEM((depth, width), jnp.bfloat16),
                pltpu.SemaphoreType.DMA,
            ],
        ),
        cost_estimate=pl.CostEstimate(flops=0, bytes_accessed=4 * depth * width, transcendentals=0),
        name="reorder",
    )(slot, panel)


def shift_kernel(scalars, *refs, parts, lags):
    pieces, out, source = refs[:parts], refs[parts], refs[parts + 1]
    blocks, length, _ = source.shape
    size = pieces[0].shape[0]
    snapshots = parts * size

    @pl.when(pl.program_id(0) == 0)
    def _():
        for j in range(blocks):
            columns = slice(j * LANES, (j + 1) * LANES)
            for m, piece in enumerate(pieces):
                start = pl.multiple_of((scalars[lags] ^ m) * size, size)
                source[j, pl.ds(start, size), :] = piece[:, columns].astype(jnp.float32)
            source[j, snapshots:, :] = jnp.zeros((length - snapshots, LANES), jnp.float32)

    offset = scalars[pl.program_id(0)]
    step = 128

    def body(i, carry):
        first = pl.multiple_of(i * step, step)
        for j in range(blocks):
            out[0, pl.ds(first, step), j * LANES : (j + 1) * LANES] = source[
                j, pl.ds(first + offset, step), :
            ].astype(jnp.bfloat16)
        return carry

    lax.fori_loop(0, snapshots // step, body, 0)


def shifted_copies(pieces, lag_offsets, mine):
    size, width = pieces[0].shape
    parts = len(pieces)
    snapshots = size * parts
    lags = lag_offsets.shape[0]
    scalars = jnp.concatenate([lag_offsets, mine.astype(jnp.int32)[None]])
    whole = pl.BlockSpec((size, width), lambda l, s: (0, 0))
    return pl.pallas_call(
        functools.partial(shift_kernel, parts=parts, lags=lags),
        out_shape=jax.ShapeDtypeStruct((lags, snapshots, width), jnp.bfloat16),
        grid_spec=pltpu.PrefetchScalarGridSpec(
            num_scalar_prefetch=1,
            grid=(lags,),
            in_specs=[whole] * parts,
            out_specs=pl.BlockSpec((1, snapshots, width), lambda l, s: (l, 0, 0)),
            scratch_shapes=[pltpu.VMEM((width // LANES, snapshots + MAXLAG + ROWS, LANES), jnp.float32)],
        ),
        cost_estimate=pl.CostEstimate(
            flops=0, bytes_accessed=2 * snapshots * width * (lags + 1), transcendentals=0
        ),
        name="shift",
    )(scalars, *pieces)


def correlate_kernel(scalars, factors, *refs, parts, size):
    pieces, shifted, out, turned = refs[:parts], refs[parts], refs[-2], refs[-1]

    @pl.when(pl.program_id(0) == 0)
    def _():
        for m, piece in enumerate(pieces):
            start = pl.multiple_of((scalars[0] ^ m) * size, size)
            turned[:, pl.ds(start, size)] = piece[...].T

    product = jnp.dot(turned[...], shifted[0], preferred_element_type=jnp.float32)
    out[0] = product * factors[pl.program_id(0)]


def correlate(pieces, shifted, factors, mine, owner, out_shape, previous):
    size, modes = pieces[0].shape
    parts = len(pieces)
    lags, snapshots, width = shifted.shape
    scalars = jnp.stack([mine, owner]).astype(jnp.int32)
    in_specs = [pl.BlockSpec((size, modes), lambda l, s, f: (0, 0))] * parts
    in_specs.append(pl.BlockSpec((1, snapshots, width), lambda l, s, f: (l, 0, 0)))
    operands = [*pieces, shifted]
    aliases = {}
    if previous is not None:
        aliases = {len(operands) + 2: 0}
        operands.append(previous)
        in_specs.append(pl.BlockSpec(memory_space=pl.ANY))
    return pl.pallas_call(
        functools.partial(correlate_kernel, parts=parts, size=size),
        out_shape=jax.ShapeDtypeStruct(out_shape, jnp.float32),
        grid_spec=pltpu.PrefetchScalarGridSpec(
            num_scalar_prefetch=2,
            grid=(lags,),
            in_specs=in_specs,
            out_specs=pl.BlockSpec((1, modes, width), lambda l, s, f: (l, s[1], 0)),
            scratch_shapes=[pltpu.VMEM((modes, snapshots), jnp.bfloat16)],
        ),
        input_output_aliases=aliases,
        cost_estimate=pl.CostEstimate(
            flops=2 * lags * modes * snapshots * width,
            bytes_accessed=lags * width * (2 * snapshots + 4 * modes),
            transcendentals=0,
        ),
        name="correlate",
    )(scalars, factors, *operands)


def reduce_scatter(pieces):
    ranks = len(pieces)
    bits = [1 << b for b in range(ranks.bit_length() - 1)]
    width = pieces[0].shape[1]
    halves = []
    for half, order in enumerate((bits, bits[::-1])):
        columns = slice(half * width // 2, (half + 1) * width // 2)
        held = [piece[:, columns] for piece in pieces]
        live = range(ranks)
        for bit in order:
            for m in reversed(live):
                if m & bit:
                    held[m ^ bit] = held[m ^ bit] + swap(held[m], "row", bit)
            live = [m for m in live if not m & bit]
        halves.append(held[0])
    return halves


def local(velocities, modes_panel, atom_slot, lag_offsets):
    ranks = lax.axis_size("row")
    columns = lax.axis_size("col")
    owners = columns // ranks
    mine = lax.axis_index("row")
    group = lax.axis_index("col") // owners
    member = lax.axis_index("col") % owners
    snapshots = velocities.shape[0]
    size = snapshots // ranks
    width = modes_panel.shape[1]
    modes = width * columns

    panel = reorder(modes_panel, atom_slot)
    pieces = [None] * ranks
    for m in reversed(range(ranks)):
        rows = lax.dynamic_slice_in_dim(velocities, (mine ^ m) * size, size, 0)
        pieces[m] = jnp.dot(rows, panel, preferred_element_type=jnp.float32)
    halves = reduce_scatter(pieces)

    energy = sum(jnp.sum(half * half, axis=1) for half in halves)
    bit = 1
    while bit < columns:
        energy = energy + swap(energy, "col", bit)
        bit *= 2
    scale = lax.rsqrt(energy / modes + epsilon)[:, None]
    own = jnp.concatenate([(half * scale).astype(jnp.bfloat16) for half in halves], axis=1)

    across = [own] + [swap(own, "col", owners * m) for m in range(1, ranks)]
    column_pieces = [own] + [swap(own, "row", m) for m in range(1, ranks)]
    shifted = shifted_copies(column_pieces, lag_offsets, mine)

    stacked = jnp.stack(across)
    row_pieces = []
    for m in range(ranks):
        chosen = lax.dynamic_index_in_dim(stacked, group ^ mine ^ m, 0, keepdims=False)
        row_pieces.append(chosen if m == 0 else swap(chosen, "row", m))

    factors = lax.rsqrt((snapshots - lag_offsets).astype(jnp.float32))
    out_shape = (lag_offsets.shape[0], width * owners, width)
    others = [[swap(piece, "col", k) for piece in row_pieces] for k in range(1, owners)]
    result = correlate(row_pieces, shifted, factors, mine, member, out_shape, None)
    for k in range(1, owners):
        result = correlate(others[k - 1], shifted, factors, mine, member ^ k, out_shape, result)
    return result


def solution(mesh):
    return jax.shard_map(
        local,
        mesh=mesh,
        in_specs=(P(None, "row"), P("row", "col"), P("row"), P()),
        out_specs=P(None, "row", "col"),
        check_vma=False,
    )
```

```python
import functools

import jax
import jax.numpy as jnp
from jax import lax
from jax.experimental import pallas as pl
from jax.experimental.pallas import tpu as pltpu
from jax.sharding import PartitionSpec as P

MAXLAG = 256
LANES = 128
ROWS = 8
GROUP = 16

epsilon = 1e-06


def swap(block, axis, offset):
    size = lax.axis_size(axis)
    return lax.ppermute(block, axis, [(i, i ^ offset) for i in range(size)])


def reorder_chunk(slot, source, ordered, chunk, c):
    blocks = source.shape[0]
    row = lax.broadcasted_iota(jnp.int32, (ROWS, LANES), 0)
    groups = chunk // (3 * GROUP)

    def move(g, carry):
        g = c * groups + g
        base = [slot[g * GROUP + i] for i in range(GROUP)]
        for j in range(blocks):
            tiles = []
            for v in range(3 * GROUP // ROWS):
                tile = None
                for i in range(GROUP):
                    low = 3 * i - ROWS * v
                    if low + 3 <= 0 or low >= ROWS:
                        continue
                    piece = source[j, pl.ds(base[i] + (ROWS - low), ROWS), :]
                    tile = piece if tile is None else jnp.where(row >= low, piece, tile)
                tiles.append(tile)
            ordered[
                pl.ds(pl.multiple_of(g * 3 * GROUP, GROUP), 3 * GROUP), j * LANES : (j + 1) * LANES
            ] = jnp.concatenate(tiles, axis=0).astype(jnp.bfloat16)
        return carry

    lax.fori_loop(0, groups, move, 0, unroll=2)


def write_turned(total, outs):
    half, size = outs[0].shape
    for i in range(len(outs) // 2):
        for h in range(2):
            outs[2 * i + h][...] = total[i * size : (i + 1) * size, h * half : (h + 1) * half].T


def reorder_project_kernel(slot, starts, panel, velocities, *refs, chunk, count):
    outs, ordered_out = refs[: 2 * count], refs[2 * count]
    staged, source, rows, total, in_sems, row_sems, out_sem = refs[2 * count + 1 :]
    depth, width = panel.shape
    blocks = width // LANES
    size = outs[0].shape[1]
    chunks = depth // chunk

    def panel_copy(c):
        part = pl.ds(c * chunk, chunk)
        return pltpu.make_async_copy(panel.at[part, :], staged.at[part, :], in_sems.at[c])

    def row_copy(i):
        first = pl.multiple_of(starts[i], size)
        return pltpu.make_async_copy(
            velocities.at[pl.ds(first, size), :], rows.at[pl.ds(i * size, size), :], row_sems.at[i]
        )

    def ordered_copy(c):
        part = pl.ds(pl.multiple_of(c * chunk, chunk), chunk)
        return pltpu.make_async_copy(staged.at[part, :], ordered_out.at[part, :], out_sem)

    for c in range(chunks):
        panel_copy(c).start()
    for i in range(count):
        row_copy(i).start()
    for c in range(chunks):
        panel_copy(c).wait()

        def widen(i, carry):
            first = pl.multiple_of(c * chunk + i * LANES, LANES)
            for j in range(blocks):
                source[j, pl.ds(ROWS + first, LANES), :] = staged[
                    pl.ds(first, LANES), j * LANES : (j + 1) * LANES
                ].astype(jnp.float32)
            return carry

        lax.fori_loop(0, chunk // LANES, widen, 0)
    for i in range(count):
        row_copy(i).wait()
    total[...] = jnp.zeros_like(total)

    def body(c, carry):
        reorder_chunk(slot, source, staged, chunk, c)
        ordered_copy(c).start()
        part = pl.ds(pl.multiple_of(c * chunk, chunk), chunk)
        total[...] += jnp.dot(rows[:, part], staged[part, :], preferred_element_type=jnp.float32)
        return carry

    lax.fori_loop(0, chunks, body, 0)
    write_turned(total, outs)
    for c in range(chunks):
        ordered_copy(c).wait()


def reorder_project(panel, velocities, slot, starts, size):
    depth, width = panel.shape
    count = starts.shape[0]
    chunk = depth // 10
    anywhere = pl.BlockSpec(memory_space=pl.ANY)
    part = jax.ShapeDtypeStruct((width // 2, size), jnp.float32)
    *parts, ordered = pl.pallas_call(
        functools.partial(reorder_project_kernel, chunk=chunk, count=count),
        out_shape=[part] * (2 * count) + [jax.ShapeDtypeStruct((depth, width), jnp.bfloat16)],
        grid_spec=pltpu.PrefetchScalarGridSpec(
            num_scalar_prefetch=2,
            grid=(1,),
            in_specs=[anywhere] * 2,
            out_specs=[pl.BlockSpec((width // 2, size), lambda i, *_: (0, 0))] * (2 * count) + [anywhere],
            scratch_shapes=[
                pltpu.VMEM((depth, width), jnp.bfloat16),
                pltpu.VMEM((width // LANES, depth + 2 * ROWS, LANES), jnp.float32),
                pltpu.VMEM((count * size, depth), jnp.bfloat16),
                pltpu.VMEM((count * size, width), jnp.float32),
                pltpu.SemaphoreType.DMA((depth // chunk,)),
                pltpu.SemaphoreType.DMA((count,)),
                pltpu.SemaphoreType.DMA,
            ],
        ),
        cost_estimate=pl.CostEstimate(
            flops=2 * count * size * depth * width,
            bytes_accessed=2 * depth * (2 * width + count * size),
            transcendentals=0,
        ),
        name="reorder_project",
    )(slot * 3, starts, panel, velocities)
    return parts, ordered


def project_kernel(starts, panel, velocities, *refs, chunk, count):
    outs = refs[: 2 * count]
    staged, rows, total, sems = refs[2 * count :]
    depth = panel.shape[0]
    size = outs[0].shape[1]
    chunks = depth // chunk

    def copies(c):
        part = pl.ds(c * chunk, chunk)
        yield pltpu.make_async_copy(panel.at[part, :], staged.at[part, :], sems.at[c, count])
        for i in range(count):
            first = pl.multiple_of(starts[i], size)
            yield pltpu.make_async_copy(
                velocities.at[pl.ds(first, size), part], rows.at[pl.ds(i * size, size), part], sems.at[c, i]
            )

    for c in range(chunks):
        for copy in copies(c):
            copy.start()
    for c in range(chunks):
        for copy in copies(c):
            copy.wait()
        part = slice(c * chunk, (c + 1) * chunk)
        product = jnp.dot(rows[:, part], staged[part, :], preferred_element_type=jnp.float32)
        total[...] = product if c == 0 else total[...] + product
    write_turned(total, outs)


def project(ordered, velocities, starts, size):
    depth, width = ordered.shape
    count = starts.shape[0]
    chunk = depth // 5
    anywhere = pl.BlockSpec(memory_space=pl.ANY)
    return pl.pallas_call(
        functools.partial(project_kernel, chunk=chunk, count=count),
        out_shape=[jax.ShapeDtypeStruct((width // 2, size), jnp.float32)] * (2 * count),
        grid_spec=pltpu.PrefetchScalarGridSpec(
            num_scalar_prefetch=1,
            grid=(1,),
            in_specs=[anywhere] * 2,
            out_specs=[pl.BlockSpec((width // 2, size), lambda i, *_: (0, 0))] * (2 * count),
            scratch_shapes=[
                pltpu.VMEM((depth, width), jnp.bfloat16),
                pltpu.VMEM((count * size, depth), jnp.bfloat16),
                pltpu.VMEM((count * size, width), jnp.float32),
                pltpu.SemaphoreType.DMA((depth // chunk, count + 1)),
            ],
        ),
        cost_estimate=pl.CostEstimate(
            flops=2 * count * size * depth * width,
            bytes_accessed=2 * depth * (width + count * size),
            transcendentals=0,
        ),
        name="project",
    )(starts, ordered, velocities)


def shift_kernel(scalars, *refs, parts, lags):
    pieces, out, source = refs[:parts], refs[parts], refs[parts + 1]
    blocks, length, _ = source.shape
    size = pieces[0].shape[1]
    snapshots = parts * size

    @pl.when(pl.program_id(0) == 0)
    def _():
        for j in range(blocks):
            columns = slice(j * LANES, (j + 1) * LANES)
            for m, piece in enumerate(pieces):
                start = pl.multiple_of((scalars[lags] ^ m) * size, size)
                source[j, pl.ds(start, size), :] = piece[columns, :].astype(jnp.float32).T
            source[j, snapshots:, :] = jnp.zeros((length - snapshots, LANES), jnp.float32)

    offset = scalars[pl.program_id(0)]
    step = 128

    def body(i, carry):
        first = pl.multiple_of(i * step, step)
        for j in range(blocks):
            out[0, pl.ds(first, step), j * LANES : (j + 1) * LANES] = source[
                j, pl.ds(first + offset, step), :
            ].astype(jnp.bfloat16)
        return carry

    lax.fori_loop(0, snapshots // step, body, 0)


def shifted_copies(pieces, lag_offsets, mine):
    width, size = pieces[0].shape
    parts = len(pieces)
    snapshots = size * parts
    lags = lag_offsets.shape[0]
    scalars = jnp.concatenate([lag_offsets, mine.astype(jnp.int32)[None]])
    whole = pl.BlockSpec((width, size), lambda l, s: (0, 0))
    return pl.pallas_call(
        functools.partial(shift_kernel, parts=parts, lags=lags),
        out_shape=jax.ShapeDtypeStruct((lags, snapshots, width), jnp.bfloat16),
        grid_spec=pltpu.PrefetchScalarGridSpec(
            num_scalar_prefetch=1,
            grid=(lags,),
            in_specs=[whole] * parts,
            out_specs=pl.BlockSpec((1, snapshots, width), lambda l, s: (l, 0, 0)),
            scratch_shapes=[pltpu.VMEM((width // LANES, snapshots + MAXLAG + ROWS, LANES), jnp.float32)],
        ),
        cost_estimate=pl.CostEstimate(
            flops=0, bytes_accessed=2 * snapshots * width * (lags + 1), transcendentals=0
        ),
        name="shift",
    )(scalars, *pieces)


def correlate_kernel(scalars, factors, *refs, parts, owners, half):
    mine, others = refs[:parts], refs[parts : parts + owners - 1]
    shifted = refs[parts + owners - 1]
    out, turned, lagged, results, in_sems, lag_sems, out_sems = refs[-7:]
    lags = shifted.shape[0]
    modes, size = mine[0].shape
    copies = []
    for m in range(parts):
        place = pl.ds(pl.multiple_of((scalars[0] ^ m) * size, size), size)
        for k in range(owners):
            piece = mine[m] if k == 0 else others[k - 1].at[m]
            copies.append(
                pltpu.make_async_copy(piece, turned.at[pl.ds(k * modes, modes), place], in_sems.at[m, k])
            )
    for copy in copies:
        copy.start()

    def lag_copy(l):
        return pltpu.make_async_copy(shifted.at[l], lagged.at[l], lag_sems.at[l])

    def out_copies(l):
        for k in range(owners):
            first = ((scalars[1] ^ k) * 2 + half) * modes
            yield pltpu.make_async_copy(
                results.at[l, pl.ds(k * modes, modes), :],
                out.at[l, pl.ds(pl.multiple_of(first, modes), modes), :],
                out_sems.at[l, k],
            )

    for l in range(lags):
        lag_copy(l).start()
    for copy in copies:
        copy.wait()

    def body(l, carry):
        lag_copy(l).wait()
        product = jnp.dot(turned[...], lagged[l], preferred_element_type=jnp.float32)
        results[l] = product * factors[l]
        for copy in out_copies(l):
            copy.start()
        return carry

    lax.fori_loop(0, lags, body, 0)
    for l in range(lags):
        for copy in out_copies(l):
            copy.wait()


def correlate(mine, others, shifted, factors, scalars, half, out_shape, previous):
    modes, size = mine[0].shape
    parts, owners = len(mine), len(others) + 1
    lags, snapshots, width = shifted.shape
    operands = [*mine, *others, shifted]
    aliases = {}
    if previous is not None:
        aliases = {len(operands) + 2: 0}
        operands.append(previous)
    anywhere = pl.BlockSpec(memory_space=pl.ANY)
    return pl.pallas_call(
        functools.partial(correlate_kernel, parts=parts, owners=owners, half=half),
        out_shape=jax.ShapeDtypeStruct(out_shape, jnp.float32),
        grid_spec=pltpu.PrefetchScalarGridSpec(
            num_scalar_prefetch=2,
            grid=(1,),
            in_specs=[anywhere] * len(operands),
            out_specs=anywhere,
            scratch_shapes=[
                pltpu.VMEM((owners * modes, snapshots), jnp.bfloat16),
                pltpu.VMEM((lags, snapshots, width), jnp.bfloat16),
                pltpu.VMEM((lags, owners * modes, width), jnp.float32),
                pltpu.SemaphoreType.DMA((parts, owners)),
                pltpu.SemaphoreType.DMA((lags,)),
                pltpu.SemaphoreType.DMA((lags, owners)),
            ],
        ),
        input_output_aliases=aliases,
        cost_estimate=pl.CostEstimate(
            flops=2 * lags * owners * modes * snapshots * width,
            bytes_accessed=lags * width * (2 * snapshots + 4 * owners * modes),
            transcendentals=0,
        ),
        name="correlate",
    )(scalars, factors, *operands)


def reduce_scatter(held, bits):
    live = range(len(held))
    held = list(held)
    for bit in bits:
        for m in reversed(live):
            if m & bit:
                held[m ^ bit] = held[m ^ bit] + swap(held[m], "row", bit)
        live = [m for m in live if not m & bit]
    return held[0]


def local(velocities, modes_panel, atom_slot, lag_offsets):
    ranks = lax.axis_size("row")
    columns = lax.axis_size("col")
    owners = columns // ranks
    mine = lax.axis_index("row")
    group = lax.axis_index("col") // owners
    member = lax.axis_index("col") % owners
    snapshots = velocities.shape[0]
    size = snapshots // ranks
    width = modes_panel.shape[1]
    modes = width * columns

    first = jnp.stack([(mine ^ m) * size for m in reversed(range(ranks))]).astype(jnp.int32)
    near = ranks // 2
    far_parts, ordered = reorder_project(modes_panel, velocities, atom_slot, first[:near], size)
    near_parts = project(ordered, velocities, first[near:], size)
    parts = [*far_parts, *near_parts]
    bits = [1 << b for b in range(ranks.bit_length() - 1)]
    halves = [
        reduce_scatter([parts[2 * (ranks - 1 - m) + h] for m in range(ranks)], bits[::-1] if h else bits)
        for h in range(2)
    ]

    energy = sum(jnp.sum(half * half, axis=0) for half in halves)
    bit = 1
    while bit < columns:
        energy = energy + swap(energy, "col", bit)
        bit *= 2
    scale = lax.rsqrt(energy / modes + epsilon)[None, :]
    halves = [(half * scale).astype(jnp.bfloat16) for half in halves]
    own = jnp.concatenate(halves, axis=0)

    across = [[piece] + [swap(piece, "col", owners * m) for m in range(1, ranks)] for piece in halves]
    column_pieces = [own] + [swap(own, "row", m) for m in range(1, ranks)]
    shifted = shifted_copies(column_pieces, lag_offsets, mine)

    factors = lax.rsqrt((snapshots - lag_offsets).astype(jnp.float32))
    scalars = jnp.stack([mine, member]).astype(jnp.int32)
    out_shape = (lag_offsets.shape[0], width * owners, width)
    result = None
    for h in range(2):
        if h == 1:
            across[h], shifted = lax.optimization_barrier((across[h], shifted))
        stacked = jnp.stack(across[h])
        pieces = []
        for m in range(ranks):
            chosen = lax.dynamic_index_in_dim(stacked, group ^ mine ^ m, 0, keepdims=False)
            pieces.append(chosen if m == 0 else swap(chosen, "row", m))
        if h == 1:
            pieces, result = lax.optimization_barrier((pieces, result))
        joined = jnp.stack(pieces)
        others = [swap(joined, "col", k) for k in range(1, owners)]
        result = correlate(pieces, others, shifted, factors, scalars, h, out_shape, result)
    return result


def solution(mesh):
    return jax.shard_map(
        local,
        mesh=mesh,
        in_specs=(P(None, "row"), P("row", "col"), P("row"), P()),
        out_specs=P(None, "row", "col"),
        check_vma=False,
    )
```

```python
import functools

import jax
import jax.numpy as jnp
from jax import lax
from jax.experimental import pallas as pl
from jax.experimental.pallas import tpu as pltpu
from jax.sharding import PartitionSpec as P


MAXLAG = 256
LANES = 128
ROWS = 8
GROUP = 16
MARGIN = 3 << 20

epsilon = 1e-06


def swap(block, axis, offset):
    size = lax.axis_size(axis)
    return lax.ppermute(block, axis, [(i, i ^ offset) for i in range(size)])


def reorder_chunk(slot, source, ordered, chunk, c):
    blocks = source.shape[0]
    row = lax.broadcasted_iota(jnp.int32, (ROWS, LANES), 0)
    groups = chunk // (3 * GROUP)

    def move(g, carry):
        g = c * groups + g
        base = [slot[g * GROUP + i] for i in range(GROUP)]
        for j in range(blocks):
            tiles = []
            for v in range(3 * GROUP // ROWS):
                tile = None
                for i in range(GROUP):
                    low = 3 * i - ROWS * v
                    if low + 3 <= 0 or low >= ROWS:
                        continue
                    piece = source[j, pl.ds(base[i] + (ROWS - low), ROWS), :]
                    tile = piece if tile is None else jnp.where(row >= low, piece, tile)
                tiles.append(tile)
            ordered[
                pl.ds(pl.multiple_of(g * 3 * GROUP, GROUP), 3 * GROUP), j * LANES : (j + 1) * LANES
            ] = jnp.concatenate(tiles, axis=0).astype(jnp.bfloat16)
        return carry

    lax.fori_loop(0, groups, move, 0, unroll=8)


def arrangement(lists):
    left, right = lists
    order = [m for m in left if m not in right] + [m for m in left if m in right]
    order += [m for m in right if m not in left]
    runs = [(min(order.index(m) for m in held), len(held)) for held in lists]
    return order, runs


def row_starts(order, size):
    mine = lax.axis_index("row")
    return [pl.multiple_of((mine ^ m) * size, size) for m in order]


def add_products(total, rows, part, ordered, runs, size):
    half = ordered.shape[1] // 2
    for h, (first, count) in enumerate(runs):
        columns = slice(h * half, (h + 1) * half)
        total[: count * size, columns] += jnp.dot(
            rows[first * size : (first + count) * size, part],
            ordered[part, columns],
            preferred_element_type=jnp.float32,
        )


def write_turned(total, outs):
    half, size = outs[0].shape
    count = len(outs) // 2
    for h in range(2):
        for i in range(count):
            outs[h * count + i][...] = total[i * size : (i + 1) * size, h * half : (h + 1) * half].T


def reorder_project_kernel(slot, panel, velocities, *refs, chunk, order, runs):
    count = runs[0][1]
    outs, ordered_out = refs[: 2 * count], refs[2 * count]
    tripled, slots, staged, source, rows, total, slot_sem, in_sems, row_sems, out_sem = refs[2 * count + 1 :]
    depth, width = panel.shape
    blocks = width // LANES
    size = outs[0].shape[1]
    chunks = depth // chunk
    starts = row_starts(order, size)

    def panel_copy(c):
        part = pl.ds(c * chunk, chunk)
        return pltpu.make_async_copy(panel.at[part, :], staged.at[part, :], in_sems.at[c])

    def row_copy(i, c):
        part = pl.ds(pl.multiple_of(c * chunk, chunk), chunk)
        return pltpu.make_async_copy(
            velocities.at[pl.ds(starts[i], size), part],
            rows.at[pl.ds(i * size, size), part],
            row_sems.at[c, i],
        )

    def ordered_copy(c):
        part = pl.ds(pl.multiple_of(c * chunk, chunk), chunk)
        return pltpu.make_async_copy(staged.at[part, :], ordered_out.at[part, :], out_sem)

    first_copy = pltpu.make_async_copy(slot, tripled, slot_sem)
    first_copy.start()
    for c in range(chunks):
        panel_copy(c).start()
    for c in range(chunks):
        for i in range(len(order)):
            row_copy(i, c).start()
    first_copy.wait()
    tripled[...] = tripled[...] * 3
    slot_copy = pltpu.make_async_copy(tripled, slots, slot_sem)
    slot_copy.start()
    total[...] = jnp.zeros_like(total)
    for c in range(chunks):
        panel_copy(c).wait()

        def widen(i, carry):
            first = pl.multiple_of(c * chunk + i * LANES, LANES)
            for j in range(blocks):
                source[j, pl.ds(ROWS + first, LANES), :] = staged[
                    pl.ds(first, LANES), j * LANES : (j + 1) * LANES
                ].astype(jnp.float32)
            return carry

        lax.fori_loop(0, chunk // LANES, widen, 0)
    slot_copy.wait()

    def body(c, carry):
        reorder_chunk(slots, source, staged, chunk, c)
        ordered_copy(c).start()
        for i in range(len(order)):
            row_copy(i, c).wait()
        part = pl.ds(pl.multiple_of(c * chunk, chunk), chunk)
        add_products(total, rows, part, staged, runs, size)
        return carry

    lax.fori_loop(0, chunks, body, 0)
    write_turned(total, outs)
    for c in range(chunks):
        ordered_copy(c).wait()


def reorder_project(panel, velocities, slot, lists, size):
    depth, width = panel.shape
    order, runs = arrangement(lists)
    count = runs[0][1]
    chunk = depth // 10
    anywhere = pl.BlockSpec(memory_space=pl.ANY)
    part = jax.ShapeDtypeStruct((width // 2, size), jnp.float32)
    *parts, ordered = pl.pallas_call(
        functools.partial(reorder_project_kernel, chunk=chunk, order=order, runs=runs),
        out_shape=[part] * (2 * count) + [jax.ShapeDtypeStruct((depth, width), jnp.bfloat16)],
        grid=(1,),
        in_specs=[pl.BlockSpec(memory_space=pltpu.HBM)] * 3,
        out_specs=[pl.BlockSpec((width // 2, size), lambda i: (0, 0))] * (2 * count) + [anywhere],
        scratch_shapes=[
            pltpu.VMEM(slot.shape, jnp.int32),
            pltpu.SMEM(slot.shape, jnp.int32),
            pltpu.VMEM((depth, width), jnp.bfloat16),
            pltpu.VMEM((width // LANES, depth + 2 * ROWS, LANES), jnp.float32),
            pltpu.VMEM((len(order) * size, depth), jnp.bfloat16),
            pltpu.VMEM((count * size, width), jnp.float32),
            pltpu.SemaphoreType.DMA,
            pltpu.SemaphoreType.DMA((depth // chunk,)),
            pltpu.SemaphoreType.DMA((depth // chunk, len(order))),
            pltpu.SemaphoreType.DMA,
        ],
        cost_estimate=pl.CostEstimate(
            flops=2 * count * size * depth * width,
            bytes_accessed=2 * depth * (2 * width + count * size),
            transcendentals=0,
        ),
        compiler_params=pltpu.CompilerParams(
            vmem_limit_bytes=2 * depth * (3 * width + len(order) * size) + 4 * size * width * count * 3 + MARGIN
        ),
        name="reorder_project",
    )(*(pltpu.with_memory_space_constraint(x, pltpu.HBM) for x in (slot, panel, velocities)))
    return parts_by_piece(parts, order, runs), ordered


def parts_by_piece(parts, order, runs):
    return [
        {m: parts[h * count + i] for i, m in enumerate(order[first : first + count])}
        for h, (first, count) in enumerate(runs)
    ]


def project_kernel(panel, velocities, *refs, chunk, order, runs):
    count = runs[0][1]
    outs = refs[: 2 * count]
    staged, rows, total, sems = refs[2 * count :]
    depth = panel.shape[0]
    size = outs[0].shape[1]
    chunks = depth // chunk
    starts = row_starts(order, size)

    def copies(c):
        part = pl.ds(c * chunk, chunk)
        yield pltpu.make_async_copy(panel.at[part, :], staged.at[part, :], sems.at[c, len(order)])
        for i, start in enumerate(starts):
            yield pltpu.make_async_copy(
                velocities.at[pl.ds(start, size), part], rows.at[pl.ds(i * size, size), part], sems.at[c, i]
            )

    for c in range(chunks):
        for copy in copies(c):
            copy.start()
    total[...] = jnp.zeros_like(total)
    for c in range(chunks):
        for copy in copies(c):
            copy.wait()
        add_products(total, rows, slice(c * chunk, (c + 1) * chunk), staged, runs, size)
    write_turned(total, outs)


def project(ordered, velocities, lists, size):
    depth, width = ordered.shape
    order, runs = arrangement(lists)
    count = runs[0][1]
    chunk = depth // 10
    anywhere = pl.BlockSpec(memory_space=pl.ANY)
    parts = pl.pallas_call(
        functools.partial(project_kernel, chunk=chunk, order=order, runs=runs),
        out_shape=[jax.ShapeDtypeStruct((width // 2, size), jnp.float32)] * (2 * count),
        grid=(1,),
        in_specs=[anywhere, pl.BlockSpec(memory_space=pltpu.HBM)],
        out_specs=[pl.BlockSpec((width // 2, size), lambda i: (0, 0))] * (2 * count),
        scratch_shapes=[
            pltpu.VMEM((depth, width), jnp.bfloat16),
            pltpu.VMEM((len(order) * size, depth), jnp.bfloat16),
            pltpu.VMEM((count * size, width), jnp.float32),
            pltpu.SemaphoreType.DMA((depth // chunk, len(order) + 1)),
        ],
        cost_estimate=pl.CostEstimate(
            flops=2 * count * size * depth * width,
            bytes_accessed=2 * depth * (width + len(order) * size),
            transcendentals=0,
        ),
        compiler_params=pltpu.CompilerParams(
            vmem_limit_bytes=2 * depth * (width + len(order) * size) + 4 * size * width * count * 3 + MARGIN
        ),
        name="project",
    )(ordered, pltpu.with_memory_space_constraint(velocities, pltpu.HBM))
    return parts_by_piece(parts, order, runs)


def shift_kernel(offsets, *refs, parts):
    pieces, out, source = refs[:parts], refs[parts], refs[parts + 1]
    blocks, length, _ = source.shape
    size = pieces[0].shape[1]
    snapshots = parts * size

    @pl.when(pl.program_id(0) == 0)
    def _():
        for j in range(blocks):
            columns = slice(j * LANES, (j + 1) * LANES)
            for m, piece in enumerate(pieces):
                start = pl.multiple_of((lax.axis_index("row") ^ m) * size, size)
                source[j, pl.ds(start, size), :] = piece[columns, :].astype(jnp.float32).T
            source[j, snapshots:, :] = jnp.zeros((length - snapshots, LANES), jnp.float32)

    offset = offsets[pl.program_id(0)]
    step = 128

    def body(i, carry):
        first = pl.multiple_of(i * step, step)
        for j in range(blocks):
            out[0, pl.ds(first, step), j * LANES : (j + 1) * LANES] = source[
                j, pl.ds(first + offset, step), :
            ].astype(jnp.bfloat16)
        return carry

    lax.fori_loop(0, snapshots // step, body, 0)


def shifted_copies(pieces, lag_offsets):
    width, size = pieces[0].shape
    parts = len(pieces)
    snapshots = size * parts
    lags = lag_offsets.shape[0]
    whole = pl.BlockSpec((width, size), lambda l, s: (0, 0))
    return pl.pallas_call(
        functools.partial(shift_kernel, parts=parts),
        out_shape=jax.ShapeDtypeStruct((lags, snapshots, width), jnp.bfloat16),
        grid_spec=pltpu.PrefetchScalarGridSpec(
            num_scalar_prefetch=1,
            grid=(lags,),
            in_specs=[whole] * parts,
            out_specs=pl.BlockSpec((1, snapshots, width), lambda l, s: (l, 0, 0)),
            scratch_shapes=[pltpu.VMEM((width // LANES, snapshots + MAXLAG + ROWS, LANES), jnp.float32)],
        ),
        cost_estimate=pl.CostEstimate(
            flops=0, bytes_accessed=2 * snapshots * width * (lags + 1), transcendentals=0
        ),
        compiler_params=pltpu.CompilerParams(
            vmem_limit_bytes=4 * width * (snapshots + MAXLAG) + 8 * snapshots * width + MARGIN
        ),
        name="shift",
    )(lag_offsets, *pieces)


def correlate_kernel(factors, *refs, parts, owners, half):
    mine, others = refs[:parts], refs[parts : parts + owners - 1]
    shifted = refs[parts + owners - 1]
    out, turned, lagged, results, in_sems, lag_sems, out_sems = refs[-7:]
    lags = shifted.shape[0]
    modes, size = mine[0].shape
    row = lax.axis_index("row")
    member = lax.rem(lax.axis_index("col"), owners)
    copies = []
    for m in range(parts):
        place = pl.ds(pl.multiple_of((row ^ m) * size, size), size)
        for k in range(owners):
            piece = mine[m] if k == 0 else others[k - 1].at[m]
            copies.append(
                pltpu.make_async_copy(piece, turned.at[pl.ds(k * modes, modes), place], in_sems.at[m, k])
            )
    for copy in copies:
        copy.start()

    def lag_copy(l):
        return pltpu.make_async_copy(shifted.at[l], lagged.at[l], lag_sems.at[l])

    def out_copies(l):
        for k in range(owners):
            first = ((member ^ k) * 2 + half) * modes
            yield pltpu.make_async_copy(
                results.at[l, pl.ds(k * modes, modes), :],
                out.at[l, pl.ds(pl.multiple_of(first, modes), modes), :],
                out_sems.at[l, k],
            )

    for l in range(lags):
        lag_copy(l).start()
    for copy in copies:
        copy.wait()

    def body(l, carry):
        lag_copy(l).wait()
        product = jnp.dot(turned[...], lagged[l], preferred_element_type=jnp.float32)
        results[l] = product * factors[l]
        for copy in out_copies(l):
            copy.start()
        return carry

    lax.fori_loop(0, lags, body, 0)
    for l in range(lags):
        for copy in out_copies(l):
            copy.wait()


def correlate(mine, others, shifted, factors, half, out_shape, previous):
    modes, _ = mine[0].shape
    parts, owners = len(mine), len(others) + 1
    lags, snapshots, width = shifted.shape
    operands = [*mine, *others, shifted]
    aliases = {}
    if previous is not None:
        aliases = {len(operands) + 1: 0}
        operands.append(previous)
    anywhere = pl.BlockSpec(memory_space=pl.ANY)
    return pl.pallas_call(
        functools.partial(correlate_kernel, parts=parts, owners=owners, half=half),
        out_shape=jax.ShapeDtypeStruct(out_shape, jnp.float32),
        grid_spec=pltpu.PrefetchScalarGridSpec(
            num_scalar_prefetch=1,
            grid=(1,),
            in_specs=[anywhere] * len(operands),
            out_specs=anywhere,
            scratch_shapes=[
                pltpu.VMEM((owners * modes, snapshots), jnp.bfloat16),
                pltpu.VMEM((lags, snapshots, width), jnp.bfloat16),
                pltpu.VMEM((lags, owners * modes, width), jnp.float32),
                pltpu.SemaphoreType.DMA((parts, owners)),
                pltpu.SemaphoreType.DMA((lags,)),
                pltpu.SemaphoreType.DMA((lags, owners)),
            ],
        ),
        input_output_aliases=aliases,
        cost_estimate=pl.CostEstimate(
            flops=2 * lags * owners * modes * snapshots * width,
            bytes_accessed=lags * width * (2 * snapshots + 4 * owners * modes),
            transcendentals=0,
        ),
        compiler_params=pltpu.CompilerParams(
            vmem_limit_bytes=lags * width * (2 * snapshots + 4 * owners * modes)
            + 2 * owners * modes * snapshots
            + MARGIN
        ),
        name="correlate",
    )(factors, *operands)


def reduce_scatter(held, bits):
    live = range(len(held))
    held = dict(held)
    for bit in bits:
        for m in reversed(live):
            if m & bit:
                arrived = swap(held[m], "row", bit)
                held[m ^ bit] = held[m ^ bit] + arrived
        live = [m for m in live if not m & bit]
    return held[0]


def steps(velocities, modes_panel, atom_slot, lag_offsets):
    ranks = lax.axis_size("row")
    columns = lax.axis_size("col")
    owners = columns // ranks
    mine = lax.axis_index("row")
    group = lax.axis_index("col") // owners
    snapshots = velocities.shape[0]
    size = snapshots // ranks
    width = modes_panel.shape[1]
    modes = width * columns

    bits = [1 << b for b in range(ranks.bit_length() - 1)]
    orders = [bits, bits[::-1]]
    early = [[m for m in range(ranks) if m & order[0]] for order in orders]
    late = [[m for m in range(ranks) if not m & order[0]] for order in orders]
    early_parts, ordered = reorder_project(modes_panel, velocities, atom_slot, early, size)
    late_parts = project(ordered, velocities, late, size)
    halves = [reduce_scatter(early_parts[h] | late_parts[h], orders[h]) for h in range(2)]

    energy = sum(jnp.sum(half * half, axis=0) for half in halves)
    bit = 1
    while bit < columns:
        energy = energy + swap(energy, "col", bit)
        bit *= 2
    scale = lax.rsqrt(energy / modes + epsilon)[None, :]
    halves = [(half * scale).astype(jnp.bfloat16) for half in halves]
    own = jnp.concatenate(halves, axis=0)

    across = []
    for h in range(2):
        across.append([halves[h]] + [swap(halves[h], "col", owners * m) for m in range(1, ranks)])
    column_pieces = [own] + [swap(own, "row", m) for m in range(1, ranks)]
    shifted = shifted_copies(column_pieces, lag_offsets)

    factors = lax.rsqrt((snapshots - lag_offsets).astype(jnp.float32))
    out_shape = (lag_offsets.shape[0], width * owners, width)
    result = None
    for h in range(2):
        if h == 1:
            across[h], shifted = lax.optimization_barrier((across[h], shifted))
        stacked = jnp.stack(across[h])
        pieces = []
        for m in range(ranks):
            chosen = lax.dynamic_index_in_dim(stacked, group ^ mine ^ m, 0, keepdims=False)
            if m:
                chosen = swap(chosen, "row", m)
            pieces.append(chosen)
        if h == 1:
            pieces, result = lax.optimization_barrier((pieces, result))
        joined = jnp.stack(pieces)
        others = [swap(joined, "col", k) for k in range(1, owners)]
        result = correlate(pieces, others, shifted, factors, h, out_shape, result)
    return result


def solution(mesh):
    return jax.shard_map(
        steps,
        mesh=mesh,
        in_specs=(P(None, "row"), P("row", "col"), P("row"), P()),
        out_specs=P(None, "row", "col"),
        check_vma=False,
    )
```

```python
import functools

import jax
import jax.numpy as jnp
from jax import lax
from jax.experimental import pallas as pl
from jax.experimental.pallas import tpu as pltpu
from jax.sharding import PartitionSpec as P


MAXLAG = 256
LANES = 128
ROWS = 8
GROUP = 16
MARGIN = 3 << 20
STEPS = 2

epsilon = 1e-06


def swap(block, axis, offset):
    size = lax.axis_size(axis)
    return lax.ppermute(block, axis, [(i, i ^ offset) for i in range(size)])


def reorder_chunk(slot, source, ordered, chunk, c):
    blocks = source.shape[0]
    row = lax.broadcasted_iota(jnp.int32, (ROWS, LANES), 0)
    groups = chunk // (3 * GROUP)

    def move(g, carry):
        g = c * groups + g
        base = [slot[g * GROUP + i] for i in range(GROUP)]
        for j in range(blocks):
            tiles = []
            for v in range(3 * GROUP // ROWS):
                tile = None
                for i in range(GROUP):
                    low = 3 * i - ROWS * v
                    if low + 3 <= 0 or low >= ROWS:
                        continue
                    piece = source[j, pl.ds(base[i] + (ROWS - low), ROWS), :]
                    tile = piece if tile is None else jnp.where(row >= low, piece, tile)
                tiles.append(tile)
            ordered[
                pl.ds(pl.multiple_of(g * 3 * GROUP, GROUP), 3 * GROUP), j * LANES : (j + 1) * LANES
            ] = jnp.concatenate(tiles, axis=0).astype(jnp.bfloat16)
        return carry

    lax.fori_loop(0, groups, move, 0, unroll=2)


def arrangement(lists):
    left, right = lists
    order = [m for m in left if m not in right] + [m for m in left if m in right]
    order += [m for m in right if m not in left]
    runs = [(min(order.index(m) for m in held), len(held)) for held in lists]
    return order, runs


def row_starts(order, size):
    mine = lax.axis_index("row")
    return [pl.multiple_of((mine ^ m) * size, size) for m in order]


def add_products(total, rows, part, ordered, runs, size):
    half = ordered.shape[1] // 2
    for h, (first, count) in enumerate(runs):
        columns = slice(h * half, (h + 1) * half)
        total[: count * size, columns] += jnp.dot(
            rows[first * size : (first + count) * size, part],
            ordered[part, columns],
            preferred_element_type=jnp.float32,
        )


def write_turned(total, outs):
    half, size = outs[0].shape
    count = len(outs) // 2
    for h in range(2):
        for i in range(count):
            outs[h * count + i][...] = total[i * size : (i + 1) * size, h * half : (h + 1) * half].T


def reorder_project_kernel(slot, panel, velocities, *refs, chunk, block, order, runs):
    count = runs[0][1]
    outs, ordered_out = refs[: 2 * count], refs[2 * count]
    tripled, slots, staged, source, rows, total, slot_sem, in_sems, row_sems, out_sem = refs[2 * count + 1 :]
    depth, width = panel.shape
    blocks = width // LANES
    size = outs[0].shape[1]
    chunks, steps = depth // chunk, depth // block
    starts = row_starts(order, size)

    def panel_copy(c):
        part = pl.ds(c * chunk, chunk)
        return pltpu.make_async_copy(panel.at[part, :], staged.at[part, :], in_sems.at[c])

    def row_copy(i, c):
        part = pl.ds(pl.multiple_of(c * block, block), block)
        return pltpu.make_async_copy(
            velocities.at[pl.ds(starts[i], size), part],
            rows.at[pl.ds(i * size, size), part],
            row_sems.at[c, i],
        )

    def ordered_copy(c):
        part = pl.ds(pl.multiple_of(c * block, block), block)
        return pltpu.make_async_copy(staged.at[part, :], ordered_out.at[part, :], out_sem)

    first_copy = pltpu.make_async_copy(slot, tripled, slot_sem)
    first_copy.start()
    for c in range(chunks):
        panel_copy(c).start()
    first_copy.wait()
    tripled[...] = tripled[...] * 3
    slot_copy = pltpu.make_async_copy(tripled, slots, slot_sem)
    slot_copy.start()
    total[...] = jnp.zeros_like(total)
    for c in range(chunks):
        panel_copy(c).wait()

        def widen(i, carry):
            first = pl.multiple_of(c * chunk + i * LANES, LANES)
            for j in range(blocks):
                source[j, pl.ds(ROWS + first, LANES), :] = staged[
                    pl.ds(first, LANES), j * LANES : (j + 1) * LANES
                ].astype(jnp.float32)
            return carry

        lax.fori_loop(0, chunk // LANES, widen, 0)
        later = c - (chunks - steps)
        if later >= 0:
            for i in range(len(order)):
                row_copy(i, later).start()
    slot_copy.wait()

    def body(c, carry):
        reorder_chunk(slots, source, staged, block, c)
        ordered_copy(c).start()
        for i in range(len(order)):
            row_copy(i, c).wait()
        part = pl.ds(pl.multiple_of(c * block, block), block)
        add_products(total, rows, part, staged, runs, size)
        return carry

    lax.fori_loop(0, steps, body, 0)
    write_turned(total, outs)
    for c in range(steps):
        ordered_copy(c).wait()


def reorder_project(panel, velocities, slot, lists, size):
    depth, width = panel.shape
    order, runs = arrangement(lists)
    count = runs[0][1]
    chunk, block = depth // 5, depth // STEPS
    anywhere = pl.BlockSpec(memory_space=pl.ANY)
    part = jax.ShapeDtypeStruct((width // 2, size), jnp.float32)
    *parts, ordered = pl.pallas_call(
        functools.partial(reorder_project_kernel, chunk=chunk, block=block, order=order, runs=runs),
        out_shape=[part] * (2 * count) + [jax.ShapeDtypeStruct((depth, width), jnp.bfloat16)],
        grid=(1,),
        in_specs=[pl.BlockSpec(memory_space=pltpu.HBM)] * 3,
        out_specs=[pl.BlockSpec((width // 2, size), lambda i: (0, 0))] * (2 * count) + [anywhere],
        scratch_shapes=[
            pltpu.VMEM(slot.shape, jnp.int32),
            pltpu.SMEM(slot.shape, jnp.int32),
            pltpu.VMEM((depth, width), jnp.bfloat16),
            pltpu.VMEM((width // LANES, depth + 2 * ROWS, LANES), jnp.float32),
            pltpu.VMEM((len(order) * size, depth), jnp.bfloat16),
            pltpu.VMEM((count * size, width), jnp.float32),
            pltpu.SemaphoreType.DMA,
            pltpu.SemaphoreType.DMA((depth // chunk,)),
            pltpu.SemaphoreType.DMA((depth // block, len(order))),
            pltpu.SemaphoreType.DMA,
        ],
        cost_estimate=pl.CostEstimate(
            flops=2 * count * size * depth * width,
            bytes_accessed=2 * depth * (2 * width + count * size),
            transcendentals=0,
        ),
        compiler_params=pltpu.CompilerParams(
            vmem_limit_bytes=2 * depth * (3 * width + len(order) * size) + 4 * size * width * count * 3 + MARGIN
        ),
        name="reorder_project",
    )(*(pltpu.with_memory_space_constraint(x, pltpu.HBM) for x in (slot, panel, velocities)))
    return parts_by_piece(parts, order, runs), ordered


def parts_by_piece(parts, order, runs):
    return [
        {m: parts[h * count + i] for i, m in enumerate(order[first : first + count])}
        for h, (first, count) in enumerate(runs)
    ]


def project_kernel(panel, velocities, *refs, chunk, order, runs):
    count = runs[0][1]
    outs = refs[: 2 * count]
    staged, rows, total, sems = refs[2 * count :]
    depth = panel.shape[0]
    size = outs[0].shape[1]
    chunks = depth // chunk
    starts = row_starts(order, size)

    def copies(c):
        part = pl.ds(c * chunk, chunk)
        yield pltpu.make_async_copy(panel.at[part, :], staged.at[part, :], sems.at[c, len(order)])
        for i, start in enumerate(starts):
            yield pltpu.make_async_copy(
                velocities.at[pl.ds(start, size), part], rows.at[pl.ds(i * size, size), part], sems.at[c, i]
            )

    for c in range(chunks):
        for copy in copies(c):
            copy.start()
    total[...] = jnp.zeros_like(total)
    for c in range(chunks):
        for copy in copies(c):
            copy.wait()
        add_products(total, rows, slice(c * chunk, (c + 1) * chunk), staged, runs, size)
    write_turned(total, outs)


def project(ordered, velocities, lists, size):
    depth, width = ordered.shape
    order, runs = arrangement(lists)
    count = runs[0][1]
    chunk = depth // 10
    anywhere = pl.BlockSpec(memory_space=pl.ANY)
    parts = pl.pallas_call(
        functools.partial(project_kernel, chunk=chunk, order=order, runs=runs),
        out_shape=[jax.ShapeDtypeStruct((width // 2, size), jnp.float32)] * (2 * count),
        grid=(1,),
        in_specs=[anywhere, pl.BlockSpec(memory_space=pltpu.HBM)],
        out_specs=[pl.BlockSpec((width // 2, size), lambda i: (0, 0))] * (2 * count),
        scratch_shapes=[
            pltpu.VMEM((depth, width), jnp.bfloat16),
            pltpu.VMEM((len(order) * size, depth), jnp.bfloat16),
            pltpu.VMEM((count * size, width), jnp.float32),
            pltpu.SemaphoreType.DMA((depth // chunk, len(order) + 1)),
        ],
        cost_estimate=pl.CostEstimate(
            flops=2 * count * size * depth * width,
            bytes_accessed=2 * depth * (width + len(order) * size),
            transcendentals=0,
        ),
        compiler_params=pltpu.CompilerParams(
            vmem_limit_bytes=2 * depth * (width + len(order) * size) + 4 * size * width * count * 3 + MARGIN
        ),
        name="project",
    )(ordered, pltpu.with_memory_space_constraint(velocities, pltpu.HBM))
    return parts_by_piece(parts, order, runs)


def shift_kernel(offsets, *refs, parts):
    pieces, out, source = refs[:parts], refs[parts], refs[parts + 1]
    blocks, length, _ = source.shape
    size = pieces[0].shape[1]
    snapshots = parts * size

    @pl.when(pl.program_id(0) == 0)
    def _():
        for j in range(blocks):
            columns = slice(j * LANES, (j + 1) * LANES)
            for m, piece in enumerate(pieces):
                start = pl.multiple_of((lax.axis_index("row") ^ m) * size, size)
                source[j, pl.ds(start, size), :] = piece[columns, :].astype(jnp.float32).T
            source[j, snapshots:, :] = jnp.zeros((length - snapshots, LANES), jnp.float32)

    offset = offsets[pl.program_id(0)]
    step = 128

    def body(i, carry):
        first = pl.multiple_of(i * step, step)
        for j in range(blocks):
            out[0, pl.ds(first, step), j * LANES : (j + 1) * LANES] = source[
                j, pl.ds(first + offset, step), :
            ].astype(jnp.bfloat16)
        return carry

    lax.fori_loop(0, snapshots // step, body, 0)


def shifted_copies(pieces, lag_offsets):
    width, size = pieces[0].shape
    parts = len(pieces)
    snapshots = size * parts
    lags = lag_offsets.shape[0]
    whole = pl.BlockSpec((width, size), lambda l, s: (0, 0))
    return pl.pallas_call(
        functools.partial(shift_kernel, parts=parts),
        out_shape=jax.ShapeDtypeStruct((lags, snapshots, width), jnp.bfloat16),
        grid_spec=pltpu.PrefetchScalarGridSpec(
            num_scalar_prefetch=1,
            grid=(lags,),
            in_specs=[whole] * parts,
            out_specs=pl.BlockSpec((1, snapshots, width), lambda l, s: (l, 0, 0)),
            scratch_shapes=[pltpu.VMEM((width // LANES, snapshots + MAXLAG + ROWS, LANES), jnp.float32)],
        ),
        cost_estimate=pl.CostEstimate(
            flops=0, bytes_accessed=2 * snapshots * width * (lags + 1), transcendentals=0
        ),
        compiler_params=pltpu.CompilerParams(
            vmem_limit_bytes=4 * width * (snapshots + MAXLAG) + 8 * snapshots * width + MARGIN
        ),
        name="shift",
    )(lag_offsets, *pieces)


def correlate_kernel(factors, *refs, parts, owners, half):
    mine, others = refs[:parts], refs[parts : parts + owners - 1]
    shifted = refs[parts + owners - 1]
    out, turned, lagged, results, in_sems, lag_sems, out_sems = refs[-7:]
    lags = shifted.shape[0]
    modes, size = mine[0].shape
    row = lax.axis_index("row")
    member = lax.rem(lax.axis_index("col"), owners)
    copies = []
    for m in range(parts):
        place = pl.ds(pl.multiple_of((row ^ m) * size, size), size)
        for k in range(owners):
            piece = mine[m] if k == 0 else others[k - 1].at[m]
            copies.append(
                pltpu.make_async_copy(piece, turned.at[pl.ds(k * modes, modes), place], in_sems.at[m, k])
            )
    for copy in copies:
        copy.start()

    def lag_copy(l):
        return pltpu.make_async_copy(shifted.at[l], lagged.at[l], lag_sems.at[l])

    def out_copies(l):
        for k in range(owners):
            first = ((member ^ k) * 2 + half) * modes
            yield pltpu.make_async_copy(
                results.at[l, pl.ds(k * modes, modes), :],
                out.at[l, pl.ds(pl.multiple_of(first, modes), modes), :],
                out_sems.at[l, k],
            )

    for l in range(lags):
        lag_copy(l).start()
    for copy in copies:
        copy.wait()

    def body(l, carry):
        lag_copy(l).wait()
        product = jnp.dot(turned[...], lagged[l], preferred_element_type=jnp.float32)
        results[l] = product * factors[l]
        for copy in out_copies(l):
            copy.start()
        return carry

    lax.fori_loop(0, lags, body, 0)
    for l in range(lags):
        for copy in out_copies(l):
            copy.wait()


def correlate(mine, others, shifted, factors, half, out_shape, previous):
    modes, _ = mine[0].shape
    parts, owners = len(mine), len(others) + 1
    lags, snapshots, width = shifted.shape
    operands = [*mine, *others, shifted]
    aliases = {}
    if previous is not None:
        aliases = {len(operands) + 1: 0}
        operands.append(previous)
    anywhere = pl.BlockSpec(memory_space=pl.ANY)
    return pl.pallas_call(
        functools.partial(correlate_kernel, parts=parts, owners=owners, half=half),
        out_shape=jax.ShapeDtypeStruct(out_shape, jnp.float32),
        grid_spec=pltpu.PrefetchScalarGridSpec(
            num_scalar_prefetch=1,
            grid=(1,),
            in_specs=[anywhere] * len(operands),
            out_specs=anywhere,
            scratch_shapes=[
                pltpu.VMEM((owners * modes, snapshots), jnp.bfloat16),
                pltpu.VMEM((lags, snapshots, width), jnp.bfloat16),
                pltpu.VMEM((lags, owners * modes, width), jnp.float32),
                pltpu.SemaphoreType.DMA((parts, owners)),
                pltpu.SemaphoreType.DMA((lags,)),
                pltpu.SemaphoreType.DMA((lags, owners)),
            ],
        ),
        input_output_aliases=aliases,
        cost_estimate=pl.CostEstimate(
            flops=2 * lags * owners * modes * snapshots * width,
            bytes_accessed=lags * width * (2 * snapshots + 4 * owners * modes),
            transcendentals=0,
        ),
        compiler_params=pltpu.CompilerParams(
            vmem_limit_bytes=lags * width * (2 * snapshots + 4 * owners * modes)
            + 2 * owners * modes * snapshots
            + MARGIN
        ),
        name="correlate",
    )(factors, *operands)


def reduce_scatter(held, bits):
    live = range(len(held))
    held = dict(held)
    for bit in bits:
        for m in reversed(live):
            if m & bit:
                arrived = swap(held[m], "row", bit)
                held[m ^ bit] = held[m ^ bit] + arrived
        live = [m for m in live if not m & bit]
    return held[0]


def steps(velocities, modes_panel, atom_slot, lag_offsets):
    ranks = lax.axis_size("row")
    columns = lax.axis_size("col")
    owners = columns // ranks
    mine = lax.axis_index("row")
    group = lax.axis_index("col") // owners
    snapshots = velocities.shape[0]
    size = snapshots // ranks
    width = modes_panel.shape[1]
    modes = width * columns

    bits = [1 << b for b in range(ranks.bit_length() - 1)]
    orders = [bits, bits[::-1]]
    early = [[m for m in range(ranks) if m & order[0]] for order in orders]
    late = [[m for m in range(ranks) if not m & order[0]] for order in orders]
    early_parts, ordered = reorder_project(modes_panel, velocities, atom_slot, early, size)
    late_parts = project(ordered, velocities, late, size)
    halves = [reduce_scatter(early_parts[h] | late_parts[h], orders[h]) for h in range(2)]

    energy = sum(jnp.sum(half * half, axis=0) for half in halves)
    bit = 1
    while bit < columns:
        energy = energy + swap(energy, "col", bit)
        bit *= 2
    scale = lax.rsqrt(energy / modes + epsilon)[None, :]
    halves = [(half * scale).astype(jnp.bfloat16) for half in halves]
    own = jnp.concatenate(halves, axis=0)

    across = []
    for h in range(2):
        across.append([halves[h]] + [swap(halves[h], "col", owners * m) for m in range(1, ranks)])
    column_pieces = [own] + [swap(own, "row", m) for m in range(1, ranks)]
    shifted = shifted_copies(column_pieces, lag_offsets)

    factors = lax.rsqrt((snapshots - lag_offsets).astype(jnp.float32))
    out_shape = (lag_offsets.shape[0], width * owners, width)
    result = None
    for h in range(2):
        if h == 1:
            across[h], shifted = lax.optimization_barrier((across[h], shifted))
        stacked = jnp.stack(across[h])
        pieces = []
        for m in range(ranks):
            chosen = lax.dynamic_index_in_dim(stacked, group ^ mine ^ m, 0, keepdims=False)
            if m:
                chosen = swap(chosen, "row", m)
            pieces.append(chosen)
        if h == 1:
            pieces, result = lax.optimization_barrier((pieces, result))
        joined = jnp.stack(pieces)
        others = [swap(joined, "col", k) for k in range(1, owners)]
        result = correlate(pieces, others, shifted, factors, h, out_shape, result)
    return result


def solution(mesh):
    return jax.shard_map(
        steps,
        mesh=mesh,
        in_specs=(P(None, "row"), P("row", "col"), P("row"), P()),
        out_specs=P(None, "row", "col"),
        check_vma=False,
    )
```

```python
import functools

import jax
import jax.numpy as jnp
from jax import lax
from jax.experimental import pallas as pl
from jax.experimental.pallas import tpu as pltpu
from jax.sharding import PartitionSpec as P


MAXLAG = 256
LANES = 128
ROWS = 8
GROUP = 16
TERMS = 3
MARGIN = 3 << 20
STEPS = 2

epsilon = 1e-06


def swap(block, axis, offset):
    size = lax.axis_size(axis)
    return lax.ppermute(block, axis, [(i, i ^ offset) for i in range(size)])


def reorder_chunk(slot, source, ordered, chunk, c):
    blocks = source.shape[0]
    row = lax.broadcasted_iota(jnp.int32, (ROWS, LANES), 0)
    groups = chunk // (3 * GROUP)

    def move(g, carry):
        g = c * groups + g
        base = [slot[g * GROUP + i] for i in range(GROUP)]
        for j in range(blocks):
            tiles = []
            for v in range(3 * GROUP // ROWS):
                tile = None
                for i in range(GROUP):
                    low = 3 * i - ROWS * v
                    if low + 3 <= 0 or low >= ROWS:
                        continue
                    piece = source[j, pl.ds(base[i] + (ROWS - low), ROWS), :]
                    tile = piece if tile is None else jnp.where(row >= low, piece, tile)
                tiles.append(tile)
            ordered[
                pl.ds(pl.multiple_of(g * 3 * GROUP, GROUP), 3 * GROUP), j * LANES : (j + 1) * LANES
            ] = jnp.concatenate(tiles, axis=0).astype(jnp.bfloat16)
        return carry

    lax.fori_loop(0, groups, move, 0, unroll=2)


def arrangement(lists):
    left, right = lists
    order = [m for m in left if m not in right] + [m for m in left if m in right]
    order += [m for m in right if m not in left]
    runs = [(min(order.index(m) for m in held), len(held)) for held in lists]
    return order, runs


def row_starts(order, size):
    mine = lax.axis_index("row")
    return [pl.multiple_of((mine ^ m) * size, size) for m in order]


def add_products(total, rows, part, ordered, runs, size):
    half = ordered.shape[1] // 2
    for h, (first, count) in enumerate(runs):
        columns = slice(h * half, (h + 1) * half)
        total[: count * size, columns] += jnp.dot(
            rows[first * size : (first + count) * size, part],
            ordered[part, columns],
            preferred_element_type=jnp.float32,
        )


def write_turned(total, outs):
    half, size = outs[0].shape
    count = len(outs) // 2
    for h in range(2):
        for i in range(count):
            outs[h * count + i][...] = total[i * size : (i + 1) * size, h * half : (h + 1) * half].T


def reorder_project_kernel(slot, panel, velocities, *refs, chunk, block, order, runs):
    count = runs[0][1]
    outs, ordered_out = refs[: 2 * count], refs[2 * count]
    tripled, slots, staged, source, rows, total, slot_sem, in_sems, row_sems, out_sem = refs[2 * count + 1 :]
    depth, width = panel.shape
    blocks = width // LANES
    size = outs[0].shape[1]
    chunks, steps = depth // chunk, depth // block
    starts = row_starts(order, size)

    def panel_copy(c):
        part = pl.ds(c * chunk, chunk)
        return pltpu.make_async_copy(panel.at[part, :], staged.at[part, :], in_sems.at[c])

    def row_copy(i, c):
        part = pl.ds(pl.multiple_of(c * block, block), block)
        return pltpu.make_async_copy(
            velocities.at[pl.ds(starts[i], size), part],
            rows.at[pl.ds(i * size, size), part],
            row_sems.at[c, i],
        )

    def ordered_copy(c):
        part = pl.ds(pl.multiple_of(c * block, block), block)
        return pltpu.make_async_copy(staged.at[part, :], ordered_out.at[part, :], out_sem)

    first_copy = pltpu.make_async_copy(slot, tripled, slot_sem)
    first_copy.start()
    for c in range(chunks):
        panel_copy(c).start()
    first_copy.wait()
    tripled[...] = tripled[...] * 3
    slot_copy = pltpu.make_async_copy(tripled, slots, slot_sem)
    slot_copy.start()
    total[...] = jnp.zeros_like(total)
    for c in range(chunks):
        panel_copy(c).wait()

        def widen(i, carry):
            first = pl.multiple_of(c * chunk + i * LANES, LANES)
            for j in range(blocks):
                source[j, pl.ds(ROWS + first, LANES), :] = staged[
                    pl.ds(first, LANES), j * LANES : (j + 1) * LANES
                ].astype(jnp.float32)
            return carry

        lax.fori_loop(0, chunk // LANES, widen, 0)
        later = c - (chunks - steps)
        if later >= 0:
            for i in range(len(order)):
                row_copy(i, later).start()
    slot_copy.wait()

    def body(c, carry):
        reorder_chunk(slots, source, staged, block, c)
        ordered_copy(c).start()
        for i in range(len(order)):
            row_copy(i, c).wait()
        part = pl.ds(pl.multiple_of(c * block, block), block)
        add_products(total, rows, part, staged, runs, size)
        return carry

    lax.fori_loop(0, steps, body, 0)
    write_turned(total, outs)
    for c in range(steps):
        ordered_copy(c).wait()


def reorder_project(panel, velocities, slot, lists, size):
    depth, width = panel.shape
    order, runs = arrangement(lists)
    count = runs[0][1]
    chunk, block = depth // 5, depth // STEPS
    anywhere = pl.BlockSpec(memory_space=pl.ANY)
    part = jax.ShapeDtypeStruct((width // 2, size), jnp.float32)
    *parts, ordered = pl.pallas_call(
        functools.partial(reorder_project_kernel, chunk=chunk, block=block, order=order, runs=runs),
        out_shape=[part] * (2 * count) + [jax.ShapeDtypeStruct((depth, width), jnp.bfloat16)],
        grid=(1,),
        in_specs=[pl.BlockSpec(memory_space=pltpu.HBM)] * 3,
        out_specs=[pl.BlockSpec((width // 2, size), lambda i: (0, 0))] * (2 * count) + [anywhere],
        scratch_shapes=[
            pltpu.VMEM(slot.shape, jnp.int32),
            pltpu.SMEM(slot.shape, jnp.int32),
            pltpu.VMEM((depth, width), jnp.bfloat16),
            pltpu.VMEM((width // LANES, depth + 2 * ROWS, LANES), jnp.float32),
            pltpu.VMEM((len(order) * size, depth), jnp.bfloat16),
            pltpu.VMEM((count * size, width), jnp.float32),
            pltpu.SemaphoreType.DMA,
            pltpu.SemaphoreType.DMA((depth // chunk,)),
            pltpu.SemaphoreType.DMA((depth // block, len(order))),
            pltpu.SemaphoreType.DMA,
        ],
        cost_estimate=pl.CostEstimate(
            flops=2 * count * size * depth * width,
            bytes_accessed=2 * depth * (2 * width + count * size),
            transcendentals=0,
        ),
        compiler_params=pltpu.CompilerParams(
            vmem_limit_bytes=2 * depth * (3 * width + len(order) * size) + 4 * size * width * count * 3 + MARGIN
        ),
        name="reorder_project",
    )(*(pltpu.with_memory_space_constraint(x, pltpu.HBM) for x in (slot, panel, velocities)))
    return parts_by_piece(parts, order, runs), ordered


def parts_by_piece(parts, order, runs):
    return [
        {m: parts[h * count + i] for i, m in enumerate(order[first : first + count])}
        for h, (first, count) in enumerate(runs)
    ]


def project_kernel(panel, velocities, *refs, chunk, order, runs):
    count = runs[0][1]
    outs = refs[: 2 * count]
    staged, rows, total, sems = refs[2 * count :]
    depth = panel.shape[0]
    size = outs[0].shape[1]
    chunks = depth // chunk
    starts = row_starts(order, size)

    def copies(c):
        part = pl.ds(c * chunk, chunk)
        yield pltpu.make_async_copy(panel.at[part, :], staged.at[part, :], sems.at[c, len(order)])
        for i, start in enumerate(starts):
            yield pltpu.make_async_copy(
                velocities.at[pl.ds(start, size), part], rows.at[pl.ds(i * size, size), part], sems.at[c, i]
            )

    for c in range(chunks):
        for copy in copies(c):
            copy.start()
    total[...] = jnp.zeros_like(total)
    for c in range(chunks):
        for copy in copies(c):
            copy.wait()
        add_products(total, rows, slice(c * chunk, (c + 1) * chunk), staged, runs, size)
    write_turned(total, outs)


def project(ordered, velocities, lists, size):
    depth, width = ordered.shape
    order, runs = arrangement(lists)
    count = runs[0][1]
    chunk = depth // 10
    anywhere = pl.BlockSpec(memory_space=pl.ANY)
    parts = pl.pallas_call(
        functools.partial(project_kernel, chunk=chunk, order=order, runs=runs),
        out_shape=[jax.ShapeDtypeStruct((width // 2, size), jnp.float32)] * (2 * count),
        grid=(1,),
        in_specs=[anywhere, pl.BlockSpec(memory_space=pltpu.HBM)],
        out_specs=[pl.BlockSpec((width // 2, size), lambda i: (0, 0))] * (2 * count),
        scratch_shapes=[
            pltpu.VMEM((depth, width), jnp.bfloat16),
            pltpu.VMEM((len(order) * size, depth), jnp.bfloat16),
            pltpu.VMEM((count * size, width), jnp.float32),
            pltpu.SemaphoreType.DMA((depth // chunk, len(order) + 1)),
        ],
        cost_estimate=pl.CostEstimate(
            flops=2 * count * size * depth * width,
            bytes_accessed=2 * depth * (width + len(order) * size),
            transcendentals=0,
        ),
        compiler_params=pltpu.CompilerParams(
            vmem_limit_bytes=2 * depth * (width + len(order) * size) + 4 * size * width * count * 3 + MARGIN
        ),
        name="project",
    )(ordered, pltpu.with_memory_space_constraint(velocities, pltpu.HBM))
    return parts_by_piece(parts, order, runs)


def shift_kernel(offsets, *refs, parts):
    pieces, (out, source, scales) = refs[:parts], refs[parts:]
    blocks, length, _ = source.shape
    size = pieces[0].shape[1]
    snapshots = parts * size

    @pl.when(pl.program_id(0) == 0)
    def _():
        for j in range(blocks):
            columns = slice(j * LANES, (j + 1) * LANES)
            for m, piece in enumerate(pieces):
                start = pl.multiple_of((lax.axis_index("row") ^ m) * size, size)
                source[j, pl.ds(start, size), :] = piece[columns, :].astype(jnp.float32).T
            source[j, snapshots:, :] = jnp.zeros((length - snapshots, LANES), jnp.float32)
        for m, piece in enumerate(pieces):
            start = pl.multiple_of((lax.axis_index("row") ^ m) * size, size)
            terms = piece[blocks * LANES :, :].astype(jnp.float32)
            scale = sum(terms[t : t + 1, :] for t in range(TERMS))
            scales[pl.ds(start, size), :] = jnp.broadcast_to(scale, (LANES, size)).T

    offset = offsets[pl.program_id(0)]
    step = 128

    def body(i, carry):
        first = pl.multiple_of(i * step, step)
        for j in range(blocks):
            late = source[j, pl.ds(first + offset, step), :] * scales[pl.ds(first, step), :]
            out[0, pl.ds(first, step), j * LANES : (j + 1) * LANES] = late.astype(jnp.bfloat16)
        return carry

    lax.fori_loop(0, snapshots // step, body, 0)


def shifted_copies(pieces, lag_offsets):
    rows, size = pieces[0].shape
    width = rows - GROUP
    parts = len(pieces)
    snapshots = size * parts
    lags = lag_offsets.shape[0]
    whole = pl.BlockSpec((rows, size), lambda l, s: (0, 0))
    return pl.pallas_call(
        functools.partial(shift_kernel, parts=parts),
        out_shape=jax.ShapeDtypeStruct((lags, snapshots, width), jnp.bfloat16),
        grid_spec=pltpu.PrefetchScalarGridSpec(
            num_scalar_prefetch=1,
            grid=(lags,),
            in_specs=[whole] * parts,
            out_specs=pl.BlockSpec((1, snapshots, width), lambda l, s: (l, 0, 0)),
            scratch_shapes=[
                pltpu.VMEM((width // LANES, snapshots + MAXLAG + ROWS, LANES), jnp.float32),
                pltpu.VMEM((snapshots, LANES), jnp.float32),
            ],
        ),
        cost_estimate=pl.CostEstimate(
            flops=0, bytes_accessed=2 * snapshots * width * (lags + 1), transcendentals=0
        ),
        compiler_params=pltpu.CompilerParams(
            vmem_limit_bytes=4 * width * (snapshots + MAXLAG) + 8 * snapshots * width + MARGIN
        ),
        name="shift",
    )(lag_offsets, *pieces)


def correlate_kernel(factors, *refs, parts, owners, half):
    mine, others = refs[:parts], refs[parts : parts + owners - 1]
    shifted = refs[parts + owners - 1]
    out, turned, lagged, results, in_sems, lag_sems, out_sems = refs[-7:]
    lags = shifted.shape[0]
    modes, size = mine[0].shape
    row = lax.axis_index("row")
    member = lax.rem(lax.axis_index("col"), owners)
    copies = []
    for m in range(parts):
        place = pl.ds(pl.multiple_of((row ^ m) * size, size), size)
        for k in range(owners):
            piece = mine[m] if k == 0 else others[k - 1].at[m]
            copies.append(
                pltpu.make_async_copy(piece, turned.at[pl.ds(k * modes, modes), place], in_sems.at[m, k])
            )
    for copy in copies:
        copy.start()

    def lag_copy(l):
        return pltpu.make_async_copy(shifted.at[l], lagged.at[l], lag_sems.at[l])

    def out_copies(l):
        for k in range(owners):
            first = ((member ^ k) * 2 + half) * modes
            yield pltpu.make_async_copy(
                results.at[l, pl.ds(k * modes, modes), :],
                out.at[l, pl.ds(pl.multiple_of(first, modes), modes), :],
                out_sems.at[l, k],
            )

    for l in range(lags):
        lag_copy(l).start()
    for copy in copies:
        copy.wait()

    def body(l, carry):
        lag_copy(l).wait()
        product = jnp.dot(turned[...], lagged[l], preferred_element_type=jnp.float32)
        results[l] = product * factors[l]
        for copy in out_copies(l):
            copy.start()
        return carry

    lax.fori_loop(0, lags, body, 0)
    for l in range(lags):
        for copy in out_copies(l):
            copy.wait()


def correlate(mine, others, shifted, factors, half, out_shape, previous):
    modes, _ = mine[0].shape
    parts, owners = len(mine), len(others) + 1
    lags, snapshots, width = shifted.shape
    operands = [*mine, *others, shifted]
    aliases = {}
    if previous is not None:
        aliases = {len(operands) + 1: 0}
        operands.append(previous)
    anywhere = pl.BlockSpec(memory_space=pl.ANY)
    return pl.pallas_call(
        functools.partial(correlate_kernel, parts=parts, owners=owners, half=half),
        out_shape=jax.ShapeDtypeStruct(out_shape, jnp.float32),
        grid_spec=pltpu.PrefetchScalarGridSpec(
            num_scalar_prefetch=1,
            grid=(1,),
            in_specs=[anywhere] * len(operands),
            out_specs=anywhere,
            scratch_shapes=[
                pltpu.VMEM((owners * modes, snapshots), jnp.bfloat16),
                pltpu.VMEM((lags, snapshots, width), jnp.bfloat16),
                pltpu.VMEM((lags, owners * modes, width), jnp.float32),
                pltpu.SemaphoreType.DMA((parts, owners)),
                pltpu.SemaphoreType.DMA((lags,)),
                pltpu.SemaphoreType.DMA((lags, owners)),
            ],
        ),
        input_output_aliases=aliases,
        cost_estimate=pl.CostEstimate(
            flops=2 * lags * owners * modes * snapshots * width,
            bytes_accessed=lags * width * (2 * snapshots + 4 * owners * modes),
            transcendentals=0,
        ),
        compiler_params=pltpu.CompilerParams(
            vmem_limit_bytes=lags * width * (2 * snapshots + 4 * owners * modes)
            + 2 * owners * modes * snapshots
            + MARGIN
        ),
        name="correlate",
    )(factors, *operands)


def reduce_scatter(held, bits):
    live = range(len(held))
    held = dict(held)
    for bit in bits:
        for m in reversed(live):
            if m & bit:
                arrived = swap(held[m], "row", bit)
                held[m ^ bit] = held[m ^ bit] + arrived
        live = [m for m in live if not m & bit]
    return held[0]


def steps(velocities, modes_panel, atom_slot, lag_offsets):
    ranks = lax.axis_size("row")
    columns = lax.axis_size("col")
    owners = columns // ranks
    mine = lax.axis_index("row")
    group = lax.axis_index("col") // owners
    snapshots = velocities.shape[0]
    size = snapshots // ranks
    width = modes_panel.shape[1]
    modes = width * columns

    bits = [1 << b for b in range(ranks.bit_length() - 1)]
    orders = [bits, bits[::-1]]
    early = [[m for m in range(ranks) if m & order[0]] for order in orders]
    late = [[m for m in range(ranks) if not m & order[0]] for order in orders]
    early_parts, ordered = reorder_project(modes_panel, velocities, atom_slot, early, size)
    late_parts = project(ordered, velocities, late, size)
    halves = [reduce_scatter(early_parts[h] | late_parts[h], orders[h]) for h in range(2)]

    raw = [half.astype(jnp.bfloat16) for half in halves]
    across = []
    for h in range(2):
        across.append([raw[h]] + [swap(raw[h], "col", owners * m) for m in range(1, ranks)])

    energy = sum(jnp.sum(half * half, axis=0) for half in halves)
    steps_left = columns.bit_length() - 1
    for step in [*range(1, steps_left), 0]:
        arrived = swap(energy, "col", 1 << step)
        energy = energy + arrived
    scale = lax.rsqrt(energy / modes + epsilon)[None, :]
    own = [(half * scale).astype(jnp.bfloat16) for half in halves]
    rest = scale
    for _ in range(TERMS):
        term = lax.reduce_precision(rest, 8, 7)
        rest = rest - term
        own.append(term.astype(jnp.bfloat16))
    own.append(jnp.zeros((GROUP - TERMS, size), jnp.bfloat16))
    own = jnp.concatenate(own, axis=0)
    column_pieces = [own] + [swap(own, "row", m) for m in range(1, ranks)]
    shifted = shifted_copies(column_pieces, lag_offsets)

    factors = lax.rsqrt((snapshots - lag_offsets).astype(jnp.float32))
    out_shape = (lag_offsets.shape[0], width * owners, width)
    result = None
    for h in range(2):
        if h == 1:
            across[h], shifted = lax.optimization_barrier((across[h], shifted))
        stacked = jnp.stack(across[h])
        pieces = []
        for m in range(ranks):
            chosen = lax.dynamic_index_in_dim(stacked, group ^ mine ^ m, 0, keepdims=False)
            if m:
                chosen = swap(chosen, "row", m)
            pieces.append(chosen)
        if h == 1:
            pieces, result = lax.optimization_barrier((pieces, result))
        joined = jnp.stack(pieces)
        others = [swap(joined, "col", k) for k in range(1, owners)]
        result = correlate(pieces, others, shifted, factors, h, out_shape, result)
    return result


def solution(mesh):
    return jax.shard_map(
        steps,
        mesh=mesh,
        in_specs=(P(None, "row"), P("row", "col"), P("row"), P()),
        out_specs=P(None, "row", "col"),
        check_vma=False,
    )
```

```python
import functools

import jax
import jax.numpy as jnp
from jax import lax
from jax.experimental import pallas as pl
from jax.experimental.pallas import tpu as pltpu
from jax.sharding import PartitionSpec as P


MAXLAG = 256
LANES = 128
ROWS = 8
GROUP = 16
TERMS = 3
MARGIN = 3 << 20
STEPS = 2

epsilon = 1e-06


def swap(block, axis, offset):
    size = lax.axis_size(axis)
    return lax.ppermute(block, axis, [(i, i ^ offset) for i in range(size)])


def reorder_chunk(slot, source, ordered, chunk, c):
    blocks = source.shape[0]
    row = lax.broadcasted_iota(jnp.int32, (ROWS, LANES), 0)
    groups = chunk // (3 * GROUP)

    def move(g, carry):
        g = c * groups + g
        base = [slot[g * GROUP + i] for i in range(GROUP)]
        for j in range(blocks):
            tiles = []
            for v in range(3 * GROUP // ROWS):
                tile = None
                for i in range(GROUP):
                    low = 3 * i - ROWS * v
                    if low + 3 <= 0 or low >= ROWS:
                        continue
                    piece = source[j, pl.ds(base[i] + (ROWS - low), ROWS), :]
                    tile = piece if tile is None else jnp.where(row >= low, piece, tile)
                tiles.append(tile)
            ordered[
                pl.ds(pl.multiple_of(g * 3 * GROUP, GROUP), 3 * GROUP), j * LANES : (j + 1) * LANES
            ] = jnp.concatenate(tiles, axis=0).astype(jnp.bfloat16)
        return carry

    lax.fori_loop(0, groups, move, 0, unroll=2)


def arrangement(lists):
    left, right = lists
    order = [m for m in left if m not in right] + [m for m in left if m in right]
    order += [m for m in right if m not in left]
    runs = [(min(order.index(m) for m in held), len(held)) for held in lists]
    return order, runs


def row_starts(order, size):
    mine = lax.axis_index("row")
    return [pl.multiple_of((mine ^ m) * size, size) for m in order]


def add_products(total, rows, part, ordered, runs, size):
    half = ordered.shape[1] // 2
    for h, (first, count) in enumerate(runs):
        columns = slice(h * half, (h + 1) * half)
        total[: count * size, columns] += jnp.dot(
            rows[first * size : (first + count) * size, part],
            ordered[part, columns],
            preferred_element_type=jnp.float32,
        )


def write_turned(total, outs):
    half, size = outs[0].shape
    count = len(outs) // 2
    for h in range(2):
        for i in range(count):
            outs[h * count + i][...] = total[i * size : (i + 1) * size, h * half : (h + 1) * half].T


def reorder_project_kernel(slot, panel, velocities, *refs, chunk, block, order, runs):
    count = runs[0][1]
    outs, ordered = refs[: 2 * count], refs[2 * count]
    tripled, slots, staged, source, rows, total, slot_sem, in_sems, row_sems = refs[2 * count + 1 :]
    depth, width = panel.shape
    blocks = width // LANES
    size = outs[0].shape[1]
    chunks, steps = depth // chunk, depth // block
    starts = row_starts(order, size)

    def panel_copy(c):
        part = pl.ds(c * chunk, chunk)
        return pltpu.make_async_copy(panel.at[part, :], staged.at[part, :], in_sems.at[c])

    def row_copy(i, c):
        part = pl.ds(pl.multiple_of(c * block, block), block)
        return pltpu.make_async_copy(
            velocities.at[pl.ds(starts[i], size), part],
            rows.at[pl.ds(i * size, size), part],
            row_sems.at[c, i],
        )

    first_copy = pltpu.make_async_copy(slot, tripled, slot_sem)
    first_copy.start()
    for c in range(chunks):
        panel_copy(c).start()
    first_copy.wait()
    tripled[...] = tripled[...] * 3
    slot_copy = pltpu.make_async_copy(tripled, slots, slot_sem)
    slot_copy.start()
    total[...] = jnp.zeros_like(total)
    for c in range(chunks):
        panel_copy(c).wait()

        def widen(i, carry):
            first = pl.multiple_of(c * chunk + i * LANES, LANES)
            for j in range(blocks):
                source[j, pl.ds(ROWS + first, LANES), :] = staged[
                    pl.ds(first, LANES), j * LANES : (j + 1) * LANES
                ].astype(jnp.float32)
            return carry

        lax.fori_loop(0, chunk // LANES, widen, 0)
        later = c - (chunks - steps)
        if later >= 0:
            for i in range(len(order)):
                row_copy(i, later).start()
    slot_copy.wait()

    def body(c, carry):
        reorder_chunk(slots, source, ordered, block, c)
        for i in range(len(order)):
            row_copy(i, c).wait()
        part = pl.ds(pl.multiple_of(c * block, block), block)
        add_products(total, rows, part, ordered, runs, size)
        return carry

    lax.fori_loop(0, steps, body, 0)
    write_turned(total, outs)


def reorder_project(panel, velocities, slot, lists, size):
    depth, width = panel.shape
    order, runs = arrangement(lists)
    count = runs[0][1]
    chunk, block = depth // 5, depth // STEPS
    part = jax.ShapeDtypeStruct((width // 2, size), jnp.float32)
    *parts, ordered = pl.pallas_call(
        functools.partial(reorder_project_kernel, chunk=chunk, block=block, order=order, runs=runs),
        out_shape=[part] * (2 * count) + [jax.ShapeDtypeStruct((depth, width), jnp.bfloat16)],
        in_specs=[pl.BlockSpec(memory_space=pltpu.HBM)] * 3,
        out_specs=[pl.BlockSpec(memory_space=pltpu.VMEM)] * (2 * count + 1),
        scratch_shapes=[
            pltpu.VMEM(slot.shape, jnp.int32),
            pltpu.SMEM(slot.shape, jnp.int32),
            pltpu.VMEM((depth, width), jnp.bfloat16),
            pltpu.VMEM((width // LANES, depth + 2 * ROWS, LANES), jnp.float32),
            pltpu.VMEM((len(order) * size, depth), jnp.bfloat16),
            pltpu.VMEM((count * size, width), jnp.float32),
            pltpu.SemaphoreType.DMA,
            pltpu.SemaphoreType.DMA((depth // chunk,)),
            pltpu.SemaphoreType.DMA((depth // block, len(order))),
        ],
        cost_estimate=pl.CostEstimate(
            flops=2 * count * size * depth * width,
            bytes_accessed=2 * depth * (2 * width + count * size),
            transcendentals=0,
        ),
        compiler_params=pltpu.CompilerParams(
            vmem_limit_bytes=2 * depth * (3 * width + len(order) * size) + 4 * size * width * count * 3 + MARGIN
        ),
        name="reorder_project",
    )(*(pltpu.with_memory_space_constraint(x, pltpu.HBM) for x in (slot, panel, velocities)))
    return parts_by_piece(parts, order, runs), ordered


def parts_by_piece(parts, order, runs):
    return [
        {m: parts[h * count + i] for i, m in enumerate(order[first : first + count])}
        for h, (first, count) in enumerate(runs)
    ]


def project_kernel(panel, velocities, *refs, chunk, order, runs):
    count = runs[0][1]
    outs = refs[: 2 * count]
    rows, total, sems = refs[2 * count :]
    depth = panel.shape[0]
    size = outs[0].shape[1]
    chunks = depth // chunk
    starts = row_starts(order, size)

    def copies(c):
        part = pl.ds(c * chunk, chunk)
        for i, start in enumerate(starts):
            yield pltpu.make_async_copy(
                velocities.at[pl.ds(start, size), part], rows.at[pl.ds(i * size, size), part], sems.at[c, i]
            )

    for c in range(chunks):
        for copy in copies(c):
            copy.start()
    total[...] = jnp.zeros_like(total)
    for c in range(chunks):
        for copy in copies(c):
            copy.wait()
        add_products(total, rows, slice(c * chunk, (c + 1) * chunk), panel, runs, size)
    write_turned(total, outs)


def project(ordered, velocities, lists, size):
    depth, width = ordered.shape
    order, runs = arrangement(lists)
    count = runs[0][1]
    chunk = depth // 10
    parts = pl.pallas_call(
        functools.partial(project_kernel, chunk=chunk, order=order, runs=runs),
        out_shape=[jax.ShapeDtypeStruct((width // 2, size), jnp.float32)] * (2 * count),
        in_specs=[pl.BlockSpec(memory_space=pltpu.VMEM), pl.BlockSpec(memory_space=pltpu.HBM)],
        out_specs=[pl.BlockSpec(memory_space=pltpu.VMEM)] * (2 * count),
        scratch_shapes=[
            pltpu.VMEM((len(order) * size, depth), jnp.bfloat16),
            pltpu.VMEM((count * size, width), jnp.float32),
            pltpu.SemaphoreType.DMA((depth // chunk, len(order))),
        ],
        cost_estimate=pl.CostEstimate(
            flops=2 * count * size * depth * width,
            bytes_accessed=2 * depth * (width + len(order) * size),
            transcendentals=0,
        ),
        compiler_params=pltpu.CompilerParams(
            vmem_limit_bytes=2 * depth * len(order) * size + 4 * size * width * count * 3 + MARGIN
        ),
        name="project",
    )(ordered, pltpu.with_memory_space_constraint(velocities, pltpu.HBM))
    return parts_by_piece(parts, order, runs)


def shift_kernel(offsets, *refs, parts):
    pieces, (out, source, scales) = refs[:parts], refs[parts:]
    blocks, length, _ = source.shape
    size = pieces[0].shape[1]
    snapshots = parts * size

    @pl.when(pl.program_id(0) == 0)
    def _():
        for j in range(blocks):
            columns = slice(j * LANES, (j + 1) * LANES)
            for m, piece in enumerate(pieces):
                start = pl.multiple_of((lax.axis_index("row") ^ m) * size, size)
                source[j, pl.ds(start, size), :] = piece[columns, :].astype(jnp.float32).T
            source[j, snapshots:, :] = jnp.zeros((length - snapshots, LANES), jnp.float32)
        for m, piece in enumerate(pieces):
            start = pl.multiple_of((lax.axis_index("row") ^ m) * size, size)
            terms = piece[blocks * LANES :, :].astype(jnp.float32)
            scale = sum(terms[t : t + 1, :] for t in range(TERMS))
            scales[pl.ds(start, size), :] = jnp.broadcast_to(scale, (LANES, size)).T

    offset = offsets[pl.program_id(0)]
    step = 128

    def body(i, carry):
        first = pl.multiple_of(i * step, step)
        for j in range(blocks):
            late = source[j, pl.ds(first + offset, step), :] * scales[pl.ds(first, step), :]
            out[0, pl.ds(first, step), j * LANES : (j + 1) * LANES] = late.astype(jnp.bfloat16)
        return carry

    lax.fori_loop(0, snapshots // step, body, 0)


def shifted_copies(pieces, lag_offsets):
    rows, size = pieces[0].shape
    width = rows - GROUP
    parts = len(pieces)
    snapshots = size * parts
    lags = lag_offsets.shape[0]
    whole = pl.BlockSpec((rows, size), lambda l, s: (0, 0))
    return pl.pallas_call(
        functools.partial(shift_kernel, parts=parts),
        out_shape=jax.ShapeDtypeStruct((lags, snapshots, width), jnp.bfloat16),
        grid_spec=pltpu.PrefetchScalarGridSpec(
            num_scalar_prefetch=1,
            grid=(lags,),
            in_specs=[whole] * parts,
            out_specs=pl.BlockSpec((1, snapshots, width), lambda l, s: (l, 0, 0)),
            scratch_shapes=[
                pltpu.VMEM((width // LANES, snapshots + MAXLAG + ROWS, LANES), jnp.float32),
                pltpu.VMEM((snapshots, LANES), jnp.float32),
            ],
        ),
        cost_estimate=pl.CostEstimate(
            flops=0, bytes_accessed=2 * snapshots * width * (lags + 1), transcendentals=0
        ),
        compiler_params=pltpu.CompilerParams(
            vmem_limit_bytes=4 * width * (snapshots + MAXLAG) + 8 * snapshots * width + MARGIN
        ),
        name="shift",
    )(lag_offsets, *pieces)


def correlate_kernel(factors, *refs, parts, owners, half):
    mine, others = refs[:parts], refs[parts : parts + owners - 1]
    shifted = refs[parts + owners - 1]
    out, turned, results, in_sems, out_sems = refs[-5:]
    lags = shifted.shape[0]
    modes, size = mine[0].shape
    row = lax.axis_index("row")
    member = lax.rem(lax.axis_index("col"), owners)
    copies = []
    for m in range(parts):
        place = pl.ds(pl.multiple_of((row ^ m) * size, size), size)
        for k in range(owners):
            piece = mine[m] if k == 0 else others[k - 1].at[m]
            copies.append(
                pltpu.make_async_copy(piece, turned.at[pl.ds(k * modes, modes), place], in_sems.at[m, k])
            )
    for copy in copies:
        copy.start()

    def out_copies(l):
        for k in range(owners):
            first = ((member ^ k) * 2 + half) * modes
            yield pltpu.make_async_copy(
                results.at[l, pl.ds(k * modes, modes), :],
                out.at[l, pl.ds(pl.multiple_of(first, modes), modes), :],
                out_sems.at[l, k],
            )

    for copy in copies:
        copy.wait()

    def body(l, carry):
        product = jnp.dot(turned[...], shifted[l], preferred_element_type=jnp.float32)
        results[l] = product * factors[l]
        for copy in out_copies(l):
            copy.start()
        return carry

    lax.fori_loop(0, lags, body, 0)
    for l in range(lags):
        for copy in out_copies(l):
            copy.wait()


def correlate(mine, others, shifted, factors, half, out_shape, previous):
    modes, _ = mine[0].shape
    parts, owners = len(mine), len(others) + 1
    lags, snapshots, width = shifted.shape
    anywhere = pl.BlockSpec(memory_space=pl.ANY)
    operands = [*mine, *others, shifted]
    in_specs = [pl.BlockSpec(memory_space=pltpu.SMEM)] + [anywhere] * (len(operands) - 1)
    in_specs.append(pl.BlockSpec(memory_space=pltpu.VMEM))
    aliases = {}
    if previous is not None:
        aliases = {len(operands) + 1: 0}
        operands.append(previous)
        in_specs.append(anywhere)
    return pl.pallas_call(
        functools.partial(correlate_kernel, parts=parts, owners=owners, half=half),
        out_shape=jax.ShapeDtypeStruct(out_shape, jnp.float32),
        in_specs=in_specs,
        out_specs=anywhere,
        scratch_shapes=[
            pltpu.VMEM((owners * modes, snapshots), jnp.bfloat16),
            pltpu.VMEM((lags, owners * modes, width), jnp.float32),
            pltpu.SemaphoreType.DMA((parts, owners)),
            pltpu.SemaphoreType.DMA((lags, owners)),
        ],
        input_output_aliases=aliases,
        cost_estimate=pl.CostEstimate(
            flops=2 * lags * owners * modes * snapshots * width,
            bytes_accessed=lags * width * (2 * snapshots + 4 * owners * modes),
            transcendentals=0,
        ),
        compiler_params=pltpu.CompilerParams(
            vmem_limit_bytes=lags * width * 4 * owners * modes
            + 2 * owners * modes * snapshots
            + MARGIN
        ),
        name="correlate",
    )(factors, *operands)


def reduce_scatter(held, bits):
    live = range(len(held))
    held = dict(held)
    for bit in bits:
        for m in reversed(live):
            if m & bit:
                arrived = swap(held[m], "row", bit)
                held[m ^ bit] = held[m ^ bit] + arrived
        live = [m for m in live if not m & bit]
    return held[0]


def steps(velocities, modes_panel, atom_slot, lag_offsets):
    ranks = lax.axis_size("row")
    columns = lax.axis_size("col")
    owners = columns // ranks
    mine = lax.axis_index("row")
    group = lax.axis_index("col") // owners
    snapshots = velocities.shape[0]
    size = snapshots // ranks
    width = modes_panel.shape[1]
    modes = width * columns

    bits = [1 << b for b in range(ranks.bit_length() - 1)]
    orders = [bits, bits[::-1]]
    early = [[m for m in range(ranks) if m & order[0]] for order in orders]
    late = [[m for m in range(ranks) if not m & order[0]] for order in orders]
    early_parts, ordered = reorder_project(modes_panel, velocities, atom_slot, early, size)
    late_parts = project(ordered, velocities, late, size)
    halves = [reduce_scatter(early_parts[h] | late_parts[h], orders[h]) for h in range(2)]

    raw = [half.astype(jnp.bfloat16) for half in halves]
    across = []
    for h in range(2):
        across.append([raw[h]] + [swap(raw[h], "col", owners * m) for m in range(1, ranks)])

    energy = sum(jnp.sum(half * half, axis=0) for half in halves)
    steps_left = columns.bit_length() - 1
    for step in [*range(1, steps_left), 0]:
        arrived = swap(energy, "col", 1 << step)
        energy = energy + arrived
    scale = lax.rsqrt(energy / modes + epsilon)[None, :]
    own = [(half * scale).astype(jnp.bfloat16) for half in halves]
    rest = scale
    for _ in range(TERMS):
        term = lax.reduce_precision(rest, 8, 7)
        rest = rest - term
        own.append(term.astype(jnp.bfloat16))
    own.append(jnp.zeros((GROUP - TERMS, size), jnp.bfloat16))
    own = jnp.concatenate(own, axis=0)
    column_pieces = [own] + [swap(own, "row", m) for m in range(1, ranks)]
    shifted = shifted_copies(column_pieces, lag_offsets)

    factors = lax.rsqrt((snapshots - lag_offsets).astype(jnp.float32))
    out_shape = (lag_offsets.shape[0], width * owners, width)
    result = None
    for h in range(2):
        if h == 1:
            across[h], shifted = lax.optimization_barrier((across[h], shifted))
        stacked = jnp.stack(across[h])
        pieces = []
        for m in range(ranks):
            chosen = lax.dynamic_index_in_dim(stacked, group ^ mine ^ m, 0, keepdims=False)
            if m:
                chosen = swap(chosen, "row", m)
            pieces.append(chosen)
        if h == 1:
            pieces, result = lax.optimization_barrier((pieces, result))
        joined = jnp.stack(pieces)
        others = [swap(joined, "col", k) for k in range(1, owners)]
        result = correlate(pieces, others, shifted, factors, h, out_shape, result)
    return result


def solution(mesh):
    return jax.shard_map(
        steps,
        mesh=mesh,
        in_specs=(P(None, "row"), P("row", "col"), P("row"), P()),
        out_specs=P(None, "row", "col"),
        check_vma=False,
    )
```

```python
import functools

import jax
import jax.numpy as jnp
from jax import lax
from jax.experimental import pallas as pl
from jax.experimental.pallas import tpu as pltpu
from jax.sharding import PartitionSpec as P


MAXLAG = 256
LANES = 128
ROWS = 8
GROUP = 16
TERMS = 3
MARGIN = 3 << 20
STEPS = 2

epsilon = 1e-06


def swap(block, axis, offset):
    size = lax.axis_size(axis)
    return lax.ppermute(block, axis, [(i, i ^ offset) for i in range(size)])


def reorder_chunk(slot, source, ordered, chunk, c):
    blocks = source.shape[0]
    row = lax.broadcasted_iota(jnp.int32, (ROWS, LANES), 0)
    groups = chunk // (3 * GROUP)

    def move(g, carry):
        g = c * groups + g
        base = [slot[g * GROUP + i] for i in range(GROUP)]
        for j in range(blocks):
            tiles = []
            for v in range(3 * GROUP // ROWS):
                tile = None
                for i in range(GROUP):
                    low = 3 * i - ROWS * v
                    if low + 3 <= 0 or low >= ROWS:
                        continue
                    piece = source[j, pl.ds(base[i] + (ROWS - low), ROWS), :]
                    tile = piece if tile is None else jnp.where(row >= low, piece, tile)
                tiles.append(tile)
            ordered[
                pl.ds(pl.multiple_of(g * 3 * GROUP, GROUP), 3 * GROUP), j * LANES : (j + 1) * LANES
            ] = jnp.concatenate(tiles, axis=0).astype(jnp.bfloat16)
        return carry

    lax.fori_loop(0, groups, move, 0)


def arrangement(lists):
    left, right = lists
    order = [m for m in left if m not in right] + [m for m in left if m in right]
    order += [m for m in right if m not in left]
    runs = [(min(order.index(m) for m in held), len(held)) for held in lists]
    return order, runs


def row_starts(order, size):
    mine = lax.axis_index("row")
    return [pl.multiple_of((mine ^ m) * size, size) for m in order]


def add_products(total, rows, part, ordered, runs, size):
    half = ordered.shape[1] // 2
    for h, (first, count) in enumerate(runs):
        columns = slice(h * half, (h + 1) * half)
        total[: count * size, columns] += jnp.dot(
            rows[first * size : (first + count) * size, part],
            ordered[part, columns],
            preferred_element_type=jnp.float32,
        )


def write_turned(total, outs):
    half, size = outs[0].shape
    count = len(outs) // 2
    for h in range(2):
        for i in range(count):
            outs[h * count + i][...] = total[i * size : (i + 1) * size, h * half : (h + 1) * half].T


def reorder_project_kernel(slot, panel, velocities, *refs, chunk, block, order, runs):
    count = runs[0][1]
    outs, ordered = refs[: 2 * count], refs[2 * count]
    tripled, slots, staged, source, rows, total, slot_sem, in_sems, row_sems = refs[2 * count + 1 :]
    depth, width = panel.shape
    blocks = width // LANES
    size = outs[0].shape[1]
    chunks, steps = depth // chunk, depth // block
    starts = row_starts(order, size)

    def panel_copy(c):
        part = pl.ds(c * chunk, chunk)
        return pltpu.make_async_copy(panel.at[part, :], staged.at[part, :], in_sems.at[c])

    def row_copy(i, c):
        part = pl.ds(pl.multiple_of(c * block, block), block)
        return pltpu.make_async_copy(
            velocities.at[pl.ds(starts[i], size), part],
            rows.at[pl.ds(i * size, size), part],
            row_sems.at[c, i],
        )

    first_copy = pltpu.make_async_copy(slot, tripled, slot_sem)
    first_copy.start()
    for c in range(chunks):
        panel_copy(c).start()
    first_copy.wait()
    tripled[...] = tripled[...] * 3
    slot_copy = pltpu.make_async_copy(tripled, slots, slot_sem)
    slot_copy.start()
    total[...] = jnp.zeros_like(total)
    for c in range(chunks):
        panel_copy(c).wait()

        def widen(i, carry):
            first = pl.multiple_of(c * chunk + i * LANES, LANES)
            for j in range(blocks):
                source[j, pl.ds(ROWS + first, LANES), :] = staged[
                    pl.ds(first, LANES), j * LANES : (j + 1) * LANES
                ].astype(jnp.float32)
            return carry

        lax.fori_loop(0, chunk // LANES, widen, 0)
        later = c - (chunks - steps)
        if later >= 0:
            for i in range(len(order)):
                row_copy(i, later).start()
    slot_copy.wait()

    def body(c, carry):
        reorder_chunk(slots, source, ordered, block, c)
        for i in range(len(order)):
            row_copy(i, c).wait()
        part = pl.ds(pl.multiple_of(c * block, block), block)
        add_products(total, rows, part, ordered, runs, size)
        return carry

    lax.fori_loop(0, steps, body, 0)
    write_turned(total, outs)


def reorder_project(panel, velocities, slot, lists, size):
    depth, width = panel.shape
    order, runs = arrangement(lists)
    count = runs[0][1]
    chunk, block = depth // 5, depth // STEPS
    part = jax.ShapeDtypeStruct((width // 2, size), jnp.float32)
    *parts, ordered = pl.pallas_call(
        functools.partial(reorder_project_kernel, chunk=chunk, block=block, order=order, runs=runs),
        out_shape=[part] * (2 * count) + [jax.ShapeDtypeStruct((depth, width), jnp.bfloat16)],
        in_specs=[pl.BlockSpec(memory_space=pltpu.HBM)] * 3,
        out_specs=[pl.BlockSpec(memory_space=pltpu.VMEM)] * (2 * count + 1),
        scratch_shapes=[
            pltpu.VMEM(slot.shape, jnp.int32),
            pltpu.SMEM(slot.shape, jnp.int32),
            pltpu.VMEM((depth, width), jnp.bfloat16),
            pltpu.VMEM((width // LANES, depth + 2 * ROWS, LANES), jnp.float32),
            pltpu.VMEM((len(order) * size, depth), jnp.bfloat16),
            pltpu.VMEM((count * size, width), jnp.float32),
            pltpu.SemaphoreType.DMA,
            pltpu.SemaphoreType.DMA((depth // chunk,)),
            pltpu.SemaphoreType.DMA((depth // block, len(order))),
        ],
        cost_estimate=pl.CostEstimate(
            flops=2 * count * size * depth * width,
            bytes_accessed=2 * depth * (2 * width + count * size),
            transcendentals=0,
        ),
        compiler_params=pltpu.CompilerParams(
            vmem_limit_bytes=2 * depth * (3 * width + len(order) * size) + 4 * size * width * count * 3 + MARGIN
        ),
        name="reorder_project",
    )(*(pltpu.with_memory_space_constraint(x, pltpu.HBM) for x in (slot, panel, velocities)))
    return parts_by_piece(parts, order, runs), ordered


def parts_by_piece(parts, order, runs):
    return [
        {m: parts[h * count + i] for i, m in enumerate(order[first : first + count])}
        for h, (first, count) in enumerate(runs)
    ]


def project_kernel(panel, velocities, *refs, chunk, order, runs):
    count = runs[0][1]
    outs = refs[: 2 * count]
    rows, total, sems = refs[2 * count :]
    depth = panel.shape[0]
    size = outs[0].shape[1]
    chunks = depth // chunk
    starts = row_starts(order, size)

    def copies(c):
        part = pl.ds(c * chunk, chunk)
        for i, start in enumerate(starts):
            yield pltpu.make_async_copy(
                velocities.at[pl.ds(start, size), part], rows.at[pl.ds(i * size, size), part], sems.at[c, i]
            )

    for c in range(chunks):
        for copy in copies(c):
            copy.start()
    total[...] = jnp.zeros_like(total)
    for c in range(chunks):
        for copy in copies(c):
            copy.wait()
        add_products(total, rows, slice(c * chunk, (c + 1) * chunk), panel, runs, size)
    write_turned(total, outs)


def project(ordered, velocities, lists, size):
    depth, width = ordered.shape
    order, runs = arrangement(lists)
    count = runs[0][1]
    chunk = depth // 10
    parts = pl.pallas_call(
        functools.partial(project_kernel, chunk=chunk, order=order, runs=runs),
        out_shape=[jax.ShapeDtypeStruct((width // 2, size), jnp.float32)] * (2 * count),
        in_specs=[pl.BlockSpec(memory_space=pltpu.VMEM), pl.BlockSpec(memory_space=pltpu.HBM)],
        out_specs=[pl.BlockSpec(memory_space=pltpu.VMEM)] * (2 * count),
        scratch_shapes=[
            pltpu.VMEM((len(order) * size, depth), jnp.bfloat16),
            pltpu.VMEM((count * size, width), jnp.float32),
            pltpu.SemaphoreType.DMA((depth // chunk, len(order))),
        ],
        cost_estimate=pl.CostEstimate(
            flops=2 * count * size * depth * width,
            bytes_accessed=2 * depth * (width + len(order) * size),
            transcendentals=0,
        ),
        compiler_params=pltpu.CompilerParams(
            vmem_limit_bytes=2 * depth * len(order) * size + 4 * size * width * count * 3 + MARGIN
        ),
        name="project",
    )(ordered, pltpu.with_memory_space_constraint(velocities, pltpu.HBM))
    return parts_by_piece(parts, order, runs)


def shift_kernel(offsets, *refs, parts):
    pieces, (out, source, scales) = refs[:parts], refs[parts:]
    blocks, length, _ = source.shape
    size = pieces[0].shape[1]
    snapshots = parts * size

    @pl.when(pl.program_id(0) == 0)
    def _():
        for j in range(blocks):
            columns = slice(j * LANES, (j + 1) * LANES)
            for m, piece in enumerate(pieces):
                start = pl.multiple_of((lax.axis_index("row") ^ m) * size, size)
                source[j, pl.ds(start, size), :] = piece[columns, :].astype(jnp.float32).T
            source[j, snapshots:, :] = jnp.zeros((length - snapshots, LANES), jnp.float32)
        for m, piece in enumerate(pieces):
            start = pl.multiple_of((lax.axis_index("row") ^ m) * size, size)
            terms = piece[blocks * LANES :, :].astype(jnp.float32)
            scale = sum(terms[t : t + 1, :] for t in range(TERMS))
            scales[pl.ds(start, size), :] = jnp.broadcast_to(scale, (LANES, size)).T

    offset = offsets[pl.program_id(0)]
    step = 128

    def body(i, carry):
        first = pl.multiple_of(i * step, step)
        for j in range(blocks):
            late = source[j, pl.ds(first + offset, step), :] * scales[pl.ds(first, step), :]
            out[0, pl.ds(first, step), j * LANES : (j + 1) * LANES] = late.astype(jnp.bfloat16)
        return carry

    lax.fori_loop(0, snapshots // step, body, 0)


def shifted_copies(pieces, lag_offsets):
    rows, size = pieces[0].shape
    width = rows - GROUP
    parts = len(pieces)
    snapshots = size * parts
    lags = lag_offsets.shape[0]
    whole = pl.BlockSpec((rows, size), lambda l, s: (0, 0))
    return pl.pallas_call(
        functools.partial(shift_kernel, parts=parts),
        out_shape=jax.ShapeDtypeStruct((lags, snapshots, width), jnp.bfloat16),
        grid_spec=pltpu.PrefetchScalarGridSpec(
            num_scalar_prefetch=1,
            grid=(lags,),
            in_specs=[whole] * parts,
            out_specs=pl.BlockSpec((1, snapshots, width), lambda l, s: (l, 0, 0)),
            scratch_shapes=[
                pltpu.VMEM((width // LANES, snapshots + MAXLAG + ROWS, LANES), jnp.float32),
                pltpu.VMEM((snapshots, LANES), jnp.float32),
            ],
        ),
        cost_estimate=pl.CostEstimate(
            flops=0, bytes_accessed=2 * snapshots * width * (lags + 1), transcendentals=0
        ),
        compiler_params=pltpu.CompilerParams(
            vmem_limit_bytes=4 * width * (snapshots + MAXLAG) + 8 * snapshots * width + MARGIN
        ),
        name="shift",
    )(lag_offsets, *pieces)


def correlate_kernel(factors, *refs, parts, owners, half):
    mine, others = refs[:parts], refs[parts : parts + owners - 1]
    shifted = refs[parts + owners - 1]
    out, turned, results, in_sems, out_sems = refs[-5:]
    lags = shifted.shape[0]
    modes, size = mine[0].shape
    row = lax.axis_index("row")
    member = lax.rem(lax.axis_index("col"), owners)
    copies = []
    for m in range(parts):
        place = pl.ds(pl.multiple_of((row ^ m) * size, size), size)
        for k in range(owners):
            piece = mine[m] if k == 0 else others[k - 1].at[m]
            copies.append(
                pltpu.make_async_copy(piece, turned.at[pl.ds(k * modes, modes), place], in_sems.at[m, k])
            )
    for copy in copies:
        copy.start()

    def out_copies(l):
        for k in range(owners):
            first = ((member ^ k) * 2 + half) * modes
            yield pltpu.make_async_copy(
                results.at[l, pl.ds(k * modes, modes), :],
                out.at[l, pl.ds(pl.multiple_of(first, modes), modes), :],
                out_sems.at[l, k],
            )

    for copy in copies:
        copy.wait()

    def body(l, carry):
        product = jnp.dot(turned[...], shifted[l], preferred_element_type=jnp.float32)
        results[l] = product * factors[l]
        for copy in out_copies(l):
            copy.start()
        return carry

    lax.fori_loop(0, lags, body, 0)
    for l in range(lags):
        for copy in out_copies(l):
            copy.wait()


def correlate(mine, others, shifted, factors, half, out_shape, previous):
    modes, _ = mine[0].shape
    parts, owners = len(mine), len(others) + 1
    lags, snapshots, width = shifted.shape
    anywhere = pl.BlockSpec(memory_space=pl.ANY)
    operands = [*mine, *others, shifted]
    in_specs = [pl.BlockSpec(memory_space=pltpu.SMEM)] + [anywhere] * (len(operands) - 1)
    in_specs.append(pl.BlockSpec(memory_space=pltpu.VMEM))
    aliases = {}
    if previous is not None:
        aliases = {len(operands) + 1: 0}
        operands.append(previous)
        in_specs.append(anywhere)
    return pl.pallas_call(
        functools.partial(correlate_kernel, parts=parts, owners=owners, half=half),
        out_shape=jax.ShapeDtypeStruct(out_shape, jnp.float32),
        in_specs=in_specs,
        out_specs=anywhere,
        scratch_shapes=[
            pltpu.VMEM((owners * modes, snapshots), jnp.bfloat16),
            pltpu.VMEM((lags, owners * modes, width), jnp.float32),
            pltpu.SemaphoreType.DMA((parts, owners)),
            pltpu.SemaphoreType.DMA((lags, owners)),
        ],
        input_output_aliases=aliases,
        cost_estimate=pl.CostEstimate(
            flops=2 * lags * owners * modes * snapshots * width,
            bytes_accessed=lags * width * (2 * snapshots + 4 * owners * modes),
            transcendentals=0,
        ),
        compiler_params=pltpu.CompilerParams(
            vmem_limit_bytes=lags * width * 4 * owners * modes
            + 2 * owners * modes * snapshots
            + MARGIN
        ),
        name="correlate",
    )(factors, *operands)


def reduce_scatter(held, bits):
    live = range(len(held))
    held = dict(held)
    for bit in bits:
        for m in reversed(live):
            if m & bit:
                arrived = swap(held[m], "row", bit)
                held[m ^ bit] = held[m ^ bit] + arrived
        live = [m for m in live if not m & bit]
    return held[0]


def steps(velocities, modes_panel, atom_slot, lag_offsets):
    ranks = lax.axis_size("row")
    columns = lax.axis_size("col")
    owners = columns // ranks
    mine = lax.axis_index("row")
    group = lax.axis_index("col") // owners
    snapshots = velocities.shape[0]
    size = snapshots // ranks
    width = modes_panel.shape[1]
    modes = width * columns

    bits = [1 << b for b in range(ranks.bit_length() - 1)]
    orders = [bits, bits[::-1]]
    onward = [[m for m in range(ranks) if m & order[0] and m ^ order[0]] for order in orders]
    final = [[order[0]] for order in orders]
    meeting = [[m for m in range(1, ranks) if not m & order[0]] for order in orders]
    parts, ordered = reorder_project(modes_panel, velocities, atom_slot, onward, size)
    for lists in (final, meeting, [[0], [0]]):
        more = project(ordered, velocities, lists, size)
        parts = [parts[h] | more[h] for h in range(2)]
    halves = [reduce_scatter(parts[h], orders[h]) for h in range(2)]

    raw = [half.astype(jnp.bfloat16) for half in halves]
    across = []
    for h in range(2):
        across.append([raw[h]] + [swap(raw[h], "col", owners * m) for m in range(1, ranks)])

    energy = sum(jnp.sum(half * half, axis=0) for half in halves)
    steps_left = columns.bit_length() - 1
    for step in [*range(1, steps_left), 0]:
        arrived = swap(energy, "col", 1 << step)
        energy = energy + arrived
    scale = lax.rsqrt(energy / modes + epsilon)[None, :]
    own = [(half * scale).astype(jnp.bfloat16) for half in halves]
    rest = scale
    for _ in range(TERMS):
        term = lax.reduce_precision(rest, 8, 7)
        rest = rest - term
        own.append(term.astype(jnp.bfloat16))
    own.append(jnp.zeros((GROUP - TERMS, size), jnp.bfloat16))
    own = jnp.concatenate(own, axis=0)
    column_pieces = [own] + [swap(own, "row", m) for m in range(1, ranks)]
    shifted = shifted_copies(column_pieces, lag_offsets)

    factors = lax.rsqrt((snapshots - lag_offsets).astype(jnp.float32))
    out_shape = (lag_offsets.shape[0], width * owners, width)
    result = None
    for h in range(2):
        if h == 1:
            across[h], shifted = lax.optimization_barrier((across[h], shifted))
        stacked = jnp.stack(across[h])
        pieces = []
        for m in range(ranks):
            chosen = lax.dynamic_index_in_dim(stacked, group ^ mine ^ m, 0, keepdims=False)
            if m:
                chosen = swap(chosen, "row", m)
            pieces.append(chosen)
        if h == 1:
            pieces, result = lax.optimization_barrier((pieces, result))
        joined = jnp.stack(pieces)
        others = [swap(joined, "col", k) for k in range(1, owners)]
        result = correlate(pieces, others, shifted, factors, h, out_shape, result)
    return result


def solution(mesh):
    return jax.shard_map(
        steps,
        mesh=mesh,
        in_specs=(P(None, "row"), P("row", "col"), P("row"), P()),
        out_specs=P(None, "row", "col"),
        check_vma=False,
    )
```
